128 devices in a mesh: depth: 16 (over z, x), tile: 8 (over y, core).
Axes of the slice: x: 4, y: 4, z: 4, core: 2. Of those that a mesh axis runs over, the one named last changes fastest.
Arguments:
- phase_map: float32 [64, 2048, 256], P('depth', 'tile'), may hold values from -3.140625 to 3.140625
- absorb: float32 [64, 2048, 256], P('depth', 'tile'), may hold values from 0.01 to 0.1
- probe_wave: float32 [2, 128, 128], replicated, may hold values from -6 to 6
- waves_in: float32 [16, 32, 2, 128, 128], P('depth', 'tile'), may hold values from -6 to 6
- scan_rows: int32 [18, 32], P(None, 'tile'), may hold values from 0 to 2047, as said below
- scan_cols: int32 [18, 32], P(None, 'tile'), may hold values from 0 to 128
Outputs:
- leaving: float32 [3, 16, 32, 2, 128, 128], P(None, 'depth', 'tile')
The draws below stay inside these ranges and needn't reach their ends.
Inputs may be any that keep to these rules, and one draw needn't show every extreme that they name: The row scan_rows[b, p] lies among the 256 object rows of the tile that holds probe p, that is between (p // 4) * 256 and that plus 256 - 1; in batch 0 every tile's first probe starts at its tile's first row and its second probe at its tile's last row.
All inputs are finite; a program needn't handle non-finite values.
Results may differ from the reference program's by a relative error of at most 0.00026.
Values sent between devices are 32-bit elements; how exact they have to be, the bound alone decides.
No kernel may reach another device: no remote copies, remote signals or barrier semaphores. Data moves between devices by JAX's collectives and lax.ppermute only.
A program may use at most 128 MiB of HBM per device.

```python
import math
import jax
import jax.numpy as jnp
from jax import lax

PATCH = 128
SL_DEV = 4
TICKS = 3
TILE_ROWS = 256
COLS = 256
PROBE_DEV = 4
SLICES = 64
ROWS = 2048
PROBES = 32
BATCHES = 18
N_DEPTH = 16


def draw_scan_rows(key, part):
    offsets = jax.random.randint(key, (BATCHES, PROBES), 0, TILE_ROWS, dtype=jnp.int32)
    probe_ids = jnp.arange(PROBES, dtype=jnp.int32)
    owners = probe_ids // PROBE_DEV
    places = probe_ids % PROBE_DEV
    batch_ids = jnp.arange(BATCHES, dtype=jnp.int32)[:, None]
    offsets = jnp.where((batch_ids == 0) & (places[None, :] == 0), 0, offsets)
    offsets = jnp.where((batch_ids == 0) & (places[None, :] == 1), TILE_ROWS - 1, offsets)
    return owners[None, :] * TILE_ROWS + offsets


def touch_ends(entries, own_key, low, top_value):
    index_at = [jax.random.randint(jax.random.fold_in(own_key, axis), (), 0, length) for axis, length in enumerate(entries.shape)]
    longest = entries.shape.index(max(entries.shape))
    beside = index_at[:longest] + [(index_at[longest] + 1) % entries.shape[longest]] + index_at[longest + 1:]
    return entries.at[tuple(index_at)].set(low).at[tuple(beside)].set(top_value)


def shard_levels(stream_key, extent, shards, low, top_value):
    gain = 1.0
    for axis_at, blocks in shards:
        draws = jax.random.uniform(jax.random.fold_in(jax.random.fold_in(stream_key, 6), axis_at), (blocks,), jnp.float32, low / len(shards), top_value / len(shards))
        gain = gain * jnp.repeat(jnp.exp(draws), extent[axis_at] // blocks).reshape((-1,) + (1,) * (len(extent) - 1 - axis_at))
    return gain


def normal_values(key, extent, deviation, limit, shards=(), kind=jnp.bfloat16):
    array = deviation * jax.random.normal(key, extent, jnp.float32)
    if shards:
        array = array * shard_levels(key, extent, shards, -0.22, 0.18)
    return jnp.clip(array, -limit, limit).astype(kind)


def setup_inputs(seed: int = 0) -> dict:
    arg_keys = jax.random.split(jax.random.key(seed), 7)
    return {
        "phase_map": jnp.clip(jax.random.uniform(arg_keys[0], (SLICES, ROWS, COLS), jnp.float32, -3.140625, 3.140625), -3.140625, 3.140625),
        "absorb": jnp.clip(jnp.exp(math.log(0.1) - 2.3025851 * jax.random.uniform(arg_keys[1], (SLICES, ROWS, COLS), jnp.float32) ** shard_levels(arg_keys[1], (SLICES, ROWS, COLS), ((0, 16), (1, 8)), -0.2, 0.2)), 0.01, 0.1),
        "probe_wave": normal_values(arg_keys[2], (2, PATCH, PATCH), 1.0, 6.0, (), jnp.float32),
        "waves_in": normal_values(arg_keys[3], (N_DEPTH, PROBES, 2, PATCH, PATCH), 1.0, 6.0, ((0, 16), (1, 8)), jnp.float32),
        "scan_rows": draw_scan_rows(jax.random.fold_in(arg_keys[6], 71), 0),
        "scan_cols": touch_ends(jax.random.randint(arg_keys[5], (BATCHES, PROBES), 0, COLS - PATCH + 1), jax.random.fold_in(arg_keys[5], 1), 0, COLS - PATCH).astype(jnp.int32),
    }


fresnel = 0.1


def propagator(patch_size):
    index_vec = jnp.arange(patch_size, dtype=jnp.int32)
    frequency = jnp.where(index_vec < patch_size // 2, index_vec, index_vec - patch_size).astype(jnp.float32)
    squared = frequency[:, None] ** 2 + frequency[None, :] ** 2
    angles = (-fresnel * math.pi / patch_size) * squared
    return jnp.cos(angles), jnp.sin(angles)


def transmission(phase_map, absorb):
    damping = jnp.exp(-absorb)
    return jnp.stack([damping * jnp.cos(phase_map), damping * jnp.sin(phase_map)], 1)


def reference(phase_map, absorb, probe_wave, waves_in, scan_rows, scan_cols):
    trans = transmission(phase_map, absorb)
    extended = jnp.concatenate([trans, trans[:, :, :PATCH]], 2)
    kernel_real, kernel_imag = propagator(PATCH)
    kernel = kernel_real + 1j * kernel_imag

    def advance(current, section, batch_num):
        row_starts = scan_rows[batch_num].astype(jnp.int32)
        col_starts = scan_cols[batch_num].astype(jnp.int32)
        wavefield = current[:, 0] + 1j * current[:, 1]
        for layer_num in range(SL_DEV):
            sheet = extended[section * SL_DEV + layer_num]

            def cut_patch(row_start, col_start):
                return lax.dynamic_slice(sheet, (jnp.int32(0), row_start, col_start), (2, PATCH, PATCH))

            patches = jax.vmap(cut_patch)(row_starts, col_starts)
            wavefield = wavefield * (patches[:, 0] + 1j * patches[:, 1])
            wavefield = jnp.fft.ifft2(jnp.fft.fft2(wavefield) * kernel)
        return jnp.stack([wavefield.real, wavefield.imag], 1).astype(jnp.float32)

    current = waves_in
    results = []
    for tick_num in range(TICKS):
        outgoing = jnp.stack([advance(current[section], section, tick_num - section + N_DEPTH - 1) for section in range(N_DEPTH)])
        results.append(outgoing)
        entering = jnp.broadcast_to(probe_wave, (1, PROBES, 2, PATCH, PATCH))
        current = jnp.concatenate([entering, outgoing[:-1]], 0)
    return jnp.stack(results)
```

```python
import functools
import math

import jax
import jax.numpy as jnp
import ml_dtypes
import numpy as np
from jax import lax
from jax.experimental import pallas as pl
from jax.experimental.pallas import tpu as pltpu
from jax.sharding import PartitionSpec as P

TICKS = 3
CHUNKS = 2
RIM_CHUNKS = 2

fresnel = 0.1
VMEM_LIMIT = 24 * 1024 * 1024

SIN_TERMS = [(-1.0) ** j / math.factorial(2 * j + 1) for j in range(7)]
COS_TERMS = [(-1.0) ** j / math.factorial(2 * j) for j in range(8)]


def hop_tables(size):
    index = np.arange(size)
    frequency = np.where(index < size // 2, index, index - size).astype(np.float64)
    k = np.exp(-1j * fresnel * math.pi * frequency**2 / size)
    lag = np.fft.ifft(k)
    g = lag[(index[:, None] - index[None, :]) % size]
    right = np.block([[g.real, g.imag], [-g.imag, g.real]])
    high = right.astype(ml_dtypes.bfloat16)
    low = (right - high.astype(np.float64)).astype(ml_dtypes.bfloat16)
    right = np.stack([high, low])
    return right, np.ascontiguousarray(right.transpose(0, 2, 1))


def series(z, terms):
    total = jnp.full_like(z, terms[-1])
    for term in terms[-2::-1]:
        total = total * z + term
    return total


def transmission(phase, absorb):
    t = 0.5 * phase
    z = t * t
    s = t * series(z, SIN_TERMS)
    c = series(z, COS_TERMS)
    damping = jnp.exp(-absorb)
    return damping * (1.0 - 2.0 * (s * s)), damping * (2.0 * (s * c))


def split(x):
    high = x.astype(jnp.bfloat16)
    return high, (x - high.astype(jnp.float32)).astype(jnp.bfloat16)


def product(a, b):
    return jnp.dot(a, b, preferred_element_type=jnp.float32)


def trans_kernel(phase_ref, absorb_ref, out_ref):
    size = out_ref.shape[-1]
    rows = phase_ref.shape[1]
    step = 32

    def body(i, carry):
        at = pl.ds(pl.multiple_of(i * step, step), step)
        for layer in range(phase_ref.shape[0]):
            for half in range(2):
                cols = slice(half * size, (half + 1) * size)
                real, imag = transmission(phase_ref[layer, at, cols], absorb_ref[layer, at, cols])
                out_ref[layer, 0, half, at, :] = real
                out_ref[layer, 1, half, at, :] = imag
        return carry

    lax.fori_loop(0, rows // step, body, 0)


def section_kernel(
    tick, layers, probes, with_rim, starts, ends, with_probe, tile_rows, *refs
):
    refs = list(refs)
    rows_ref, cols_ref = refs.pop(0), refs.pop(0)
    wave_ref = refs.pop(0)
    probe_ref = refs.pop(0) if with_probe else None
    right_ref, left_ref = refs.pop(0), refs.pop(0)
    count = len(layers)
    if with_rim:
        whole_ref, rim_ref = refs.pop(0), refs.pop(0)
        out_ref = refs.pop(0)
        ext_refs = [refs.pop(0) for _ in range(count)]
    else:
        ext_refs = [refs.pop(0) for _ in range(count)]
        out_ref = refs.pop(0)
    state, x_high, x_low, r_high, r_low = refs

    size = out_ref.shape[-1]
    depth = lax.axis_index("depth")
    batch = tick - depth + lax.axis_size("depth") - 1
    offset = lax.axis_index("tile") * tile_rows
    row_at = [rows_ref[batch, p] - offset for p in probes]
    col_at = [cols_ref[batch, p] for p in probes]
    lane = lax.broadcasted_iota(jnp.int32, (size, size), 1)

    for n in range(len(probes)):
        for part in range(2):
            wave = wave_ref[n, part]
            if with_probe:
                wave = jnp.where(depth == 0, probe_ref[part], wave)
            if starts:
                wave = pltpu.roll(wave, col_at[n] & (size - 1), 1)
            state[n, part] = wave

    for j in range(count):
        ext = ext_refs[j]
        if with_rim:
            for part in range(2):
                for half in range(2):
                    ext[part, half, :tile_rows, :] = whole_ref[j, part, half]
            for half in range(2):
                cols = slice(half * size, (half + 1) * size)
                real, imag = transmission(rim_ref[0, j, :, cols], rim_ref[1, j, :, cols])
                ext[0, half, tile_rows:, :] = real
                ext[1, half, tile_rows:, :] = imag
        for n in range(len(probes)):
            at = pl.ds(row_at[n], size)
            inside = lane >= col_at[n]
            t_real = jnp.where(inside, ext[0, 0, at, :], ext[0, 1, at, :])
            t_imag = jnp.where(inside, ext[1, 0, at, :], ext[1, 1, at, :])
            real, imag = state[n, 0], state[n, 1]
            rows = slice(n * size, (n + 1) * size)
            x_high[rows, :size], x_low[rows, :size] = split(real * t_real - imag * t_imag)
            x_high[rows, size:], x_low[rows, size:] = split(real * t_imag + imag * t_real)
        y = (
            product(x_high[...], right_ref[0])
            + product(x_high[...], right_ref[1])
            + product(x_low[...], right_ref[0])
        )
        for n in range(len(probes)):
            rows = slice(n * size, (n + 1) * size)
            r_high[:size, rows], r_low[:size, rows] = split(y[rows, :size])
            r_high[size:, rows], r_low[size:, rows] = split(y[rows, size:])
        z = (
            product(left_ref[0], r_high[...])
            + product(left_ref[1], r_high[...])
            + product(left_ref[0], r_low[...])
        )
        for n in range(len(probes)):
            rows = slice(n * size, (n + 1) * size)
            for part in range(2):
                wave = z[part * size : (part + 1) * size, rows]
                if j == count - 1:
                    if ends:
                        wave = pltpu.roll(wave, (size - col_at[n]) & (size - 1), 1)
                    out_ref[n, part] = wave
                else:
                    state[n, part] = wave


def vmem():
    return pl.BlockSpec(memory_space=pltpu.VMEM)


def section(
    tick, layers, probes, scans, tables, wave, *, whole=None, rim=None, exts=None,
    probe_wave=None, starts, ends, tile_rows, name
):
    size = wave.shape[-1]
    with_rim = rim is not None
    count = len(layers)
    n = len(probes)
    operands = [*scans, wave]
    specs = [pl.BlockSpec(memory_space=pltpu.SMEM)] * 2
    first = probes[0] if wave.shape[0] != n else 0
    specs.append(pl.BlockSpec((n, 2, size, size), lambda i: (first // n, 0, 0, 0)))
    if probe_wave is not None:
        operands.append(probe_wave)
        specs.append(vmem())
    operands += list(tables)
    specs += [vmem()] * 2
    out_shape = [jax.ShapeDtypeStruct((n, 2, size, size), jnp.float32)]
    out_specs = [vmem()]
    if with_rim:
        operands += [whole, rim]
        block = layers[0] // count
        specs += [
            pl.BlockSpec((count, 2, 2, tile_rows, size), lambda i: (block, 0, 0, 0, 0)),
            vmem(),
        ]
        out_shape += [
            jax.ShapeDtypeStruct((2, 2, tile_rows + size, size), jnp.float32)
        ] * count
        out_specs += [vmem()] * count
    else:
        operands += list(exts)
        specs += [vmem()] * count
    flops = count * n * 2 * 3 * 2 * size * (2 * size) ** 2
    return pl.pallas_call(
        functools.partial(
            section_kernel, tick, layers, probes, with_rim, starts, ends,
            probe_wave is not None, tile_rows,
        ),
        grid=(1,),
        in_specs=specs,
        out_specs=out_specs,
        out_shape=out_shape,
        scratch_shapes=[
            pltpu.VMEM((n, 2, size, size), jnp.float32),
            pltpu.VMEM((n * size, 2 * size), jnp.bfloat16),
            pltpu.VMEM((n * size, 2 * size), jnp.bfloat16),
            pltpu.VMEM((2 * size, n * size), jnp.bfloat16),
            pltpu.VMEM((2 * size, n * size), jnp.bfloat16),
        ],
        compiler_params=pltpu.CompilerParams(vmem_limit_bytes=VMEM_LIMIT),
        cost_estimate=pl.CostEstimate(
            flops=flops, bytes_accessed=count * 2 * 2 * 384 * size * 4, transcendentals=0
        ),
        name=name,
    )(*operands)


def shards(phase_map, absorb, probe_wave, waves_in, scan_rows, scan_cols):
    size = probe_wave.shape[-1]
    slices, tile_rows = phase_map.shape[:2]
    tiles = lax.axis_size("tile")
    depth_count = lax.axis_size("depth")
    back = [(i, (i - 1) % tiles) for i in range(tiles)]
    onward = [(i, i + 1) for i in range(depth_count - 1)]

    per_rim = slices // RIM_CHUNKS
    rims = []
    for r in range(RIM_CHUNKS):
        at = slice(r * per_rim, (r + 1) * per_rim)
        own = jnp.stack([phase_map[at, :size], absorb[at, :size]])
        rims.append(lax.ppermute(own, "tile", back))

    tables = [jnp.asarray(table) for table in hop_tables(size)]
    scans = (scan_rows, scan_cols)
    whole = pl.pallas_call(
        trans_kernel,
        out_shape=jax.ShapeDtypeStruct((slices, 2, 2, tile_rows, size), jnp.float32),
        in_specs=[vmem()] * 2,
        out_specs=vmem(),
        compiler_params=pltpu.CompilerParams(vmem_limit_bytes=VMEM_LIMIT),
        cost_estimate=pl.CostEstimate(
            flops=slices * tile_rows * 2 * size * 40,
            bytes_accessed=slices * tile_rows * 2 * size * 16,
            transcendentals=slices * tile_rows * 2 * size,
        ),
        name="trans",
    )(phase_map, absorb)

    held = waves_in[0]
    count = held.shape[0]
    per_chunk = count // CHUNKS
    groups = [list(range(c * per_chunk, (c + 1) * per_chunk)) for c in range(CHUNKS)]
    exts = []
    for r in range(RIM_CHUNKS - 1):
        layers = list(range(r * per_rim, (r + 1) * per_rim))
        held, *made = section(
            0, layers, list(range(count)), scans, tables, held, whole=whole, rim=rims[r],
            starts=r == 0, ends=False, tile_rows=tile_rows, name=f"enter{r}",
        )
        exts += made
    results = [[]]
    layers = list(range(slices - per_rim, slices))
    for c, group in enumerate(groups):
        rest = dict(starts=RIM_CHUNKS == 1, ends=True, tile_rows=tile_rows, name=f"leave{c}")
        if c == 0:
            done, *made = section(
                0, layers, group, scans, tables, held, whole=whole, rim=rims[-1], **rest
            )
            exts += made
        else:
            (done,) = section(
                0, layers, group, scans, tables, held, exts=exts[-per_rim:], **rest
            )
        results[0].append(done)

    for tick in range(1, TICKS):
        arrived = [lax.ppermute(done, "depth", onward) for done in results[-1]]
        results.append([])
        for c, group in enumerate(groups):
            (done,) = section(
                tick, list(range(slices)), group, scans, tables, arrived[c], exts=exts,
                probe_wave=probe_wave, starts=True, ends=True, tile_rows=tile_rows,
                name=f"tick{tick}_{c}",
            )
            results[-1].append(done)
    out = jnp.stack([jnp.concatenate(parts, 0) for parts in results])
    return out[:, None]


def solution(mesh):
    return jax.shard_map(
        shards,
        mesh=mesh,
        in_specs=(
            P("depth", "tile", None),
            P("depth", "tile", None),
            P(),
            P("depth", "tile", None, None, None),
            P(None, "tile"),
            P(None, "tile"),
        ),
        out_specs=P(None, "depth", "tile", None, None, None),
        check_vma=False,
    )
```

```python
import functools
import math

import jax
import jax.numpy as jnp
import ml_dtypes
import numpy as np
from jax import lax
from jax.experimental import pallas as pl
from jax.experimental.pallas import tpu as pltpu
from jax.sharding import PartitionSpec as P

TICKS = 3
CHUNKS = 2
RIM_CHUNKS = 4

fresnel = 0.1
VMEM_LIMIT = 24 * 1024 * 1024

SIN_TERMS = [(-1.0) ** j / math.factorial(2 * j + 1) for j in range(7)]
COS_TERMS = [(-1.0) ** j / math.factorial(2 * j) for j in range(8)]


def hop_tables(size):
    index = np.arange(size)
    frequency = np.where(index < size // 2, index, index - size).astype(np.float64)
    k = np.exp(-1j * fresnel * math.pi * frequency**2 / size)
    lag = np.fft.ifft(k)
    g = lag[(index[:, None] - index[None, :]) % size]
    right = np.block([[g.real, g.imag], [-g.imag, g.real]])
    high = right.astype(ml_dtypes.bfloat16)
    low = (right - high.astype(np.float64)).astype(ml_dtypes.bfloat16)
    right = np.stack([high, low])
    return right, np.ascontiguousarray(right.transpose(0, 2, 1))


def series(z, terms):
    total = jnp.full_like(z, terms[-1])
    for term in terms[-2::-1]:
        total = total * z + term
    return total


def transmission(phase, absorb):
    t = 0.5 * phase
    z = t * t
    s = t * series(z, SIN_TERMS)
    c = series(z, COS_TERMS)
    damping = jnp.exp(-absorb)
    return damping * (1.0 - 2.0 * (s * s)), damping * (2.0 * (s * c))


def split(x):
    high = x.astype(jnp.bfloat16)
    return high, (x - high.astype(jnp.float32)).astype(jnp.bfloat16)


def product(a, b):
    return jnp.dot(a, b, preferred_element_type=jnp.float32)


def trans_kernel(phase_ref, absorb_ref, out_ref):
    size = out_ref.shape[-1]
    step = 32

    def body(i, carry):
        at = pl.ds(pl.multiple_of(i * step, step), step)
        for layer in range(phase_ref.shape[0]):
            for half in range(2):
                cols = slice(half * size, (half + 1) * size)
                real, imag = transmission(phase_ref[layer, at, cols], absorb_ref[layer, at, cols])
                out_ref[layer, 0, half, at, :] = real
                out_ref[layer, 1, half, at, :] = imag
        return carry

    lax.fori_loop(0, phase_ref.shape[1] // step, body, 0)


def trans_rows(phase_map, absorb, size, layers, block, name):
    count = len(layers)
    columns = phase_map.shape[2]
    at = layers[0] // count
    spec = pl.BlockSpec((count, size, columns), lambda i: (at, block, 0))
    values = count * size * columns
    return pl.pallas_call(
        trans_kernel,
        grid=(1,),
        out_shape=jax.ShapeDtypeStruct((count, 2, columns // size, size, size), jnp.float32),
        in_specs=[spec] * 2,
        out_specs=vmem(),
        compiler_params=pltpu.CompilerParams(vmem_limit_bytes=VMEM_LIMIT),
        cost_estimate=pl.CostEstimate(
            flops=values * 40, bytes_accessed=values * 16, transcendentals=values
        ),
        name=name,
    )(phase_map, absorb)


def store_kernel(tick, count, *refs):
    parts = refs[:count]
    out, sem = refs[-2:]
    copies = []
    at = 0
    for part in parts:
        copies.append(
            pltpu.make_async_copy(
                part, out.at[tick, pl.ds(at, part.shape[0])], sem.at[len(copies)]
            )
        )
        copies[-1].start()
        at += part.shape[0]
    for copy in copies:
        copy.wait()


def store(tick, parts, out, out_shape):
    count = len(parts)
    operands = list(parts)
    specs = [vmem()] * count
    aliases = {}
    if out is not None:
        aliases = {count: 0}
        operands.append(out)
        specs.append(pl.BlockSpec(memory_space=pltpu.HBM))
    return pl.pallas_call(
        functools.partial(store_kernel, tick, count),
        out_shape=out_shape,
        in_specs=specs,
        out_specs=pl.BlockSpec(memory_space=pltpu.HBM),
        input_output_aliases=aliases,
        scratch_shapes=[pltpu.SemaphoreType.DMA((count,))],
        compiler_params=pltpu.CompilerParams(vmem_limit_bytes=VMEM_LIMIT),
        name=f"store{tick}",
    )(*operands)


def section_kernel(
    tick, layers, probes, with_rim, starts, ends, with_probe, with_out, tile_rows, *refs
):
    refs = list(refs)
    rows_ref, cols_ref = refs.pop(0), refs.pop(0)
    wave_ref = refs.pop(0)
    probe_ref = refs.pop(0) if with_probe else None
    right_ref, left_ref = refs.pop(0), refs.pop(0)
    count = len(layers)
    if with_rim:
        piece_refs = [refs.pop(0) for _ in range(3)]
        out_ref = refs.pop(0)
        ext_refs = [refs.pop(0) for _ in range(count)]
    else:
        ext_refs = [refs.pop(0) for _ in range(count)]
        if with_out:
            refs.pop(0)
        out_ref = refs.pop(0)
    if with_out:
        final_ref = out_ref
        out_ref = refs.pop()
        sem = refs.pop()
    state, x_high, x_low, r_high, r_low = refs

    size = out_ref.shape[-1]
    depth = lax.axis_index("depth")
    batch = tick - depth + lax.axis_size("depth") - 1
    offset = lax.axis_index("tile") * tile_rows
    row_at = [rows_ref[batch, p] - offset for p in probes]
    col_at = [cols_ref[batch, p] for p in probes]
    lane = lax.broadcasted_iota(jnp.int32, (size, size), 1)

    for n in range(len(probes)):
        for part in range(2):
            wave = wave_ref[n, part]
            if with_probe:
                wave = jnp.where(depth == 0, probe_ref[part], wave)
            if starts:
                wave = pltpu.roll(wave, col_at[n] & (size - 1), 1)
            state[n, part] = wave

    for j in range(count):
        ext = ext_refs[j]
        if with_rim:
            for piece, piece_ref in enumerate(piece_refs):
                rows = slice(piece * size, (piece + 1) * size)
                for part in range(2):
                    for half in range(2):
                        ext[part, half, rows, :] = piece_ref[j, part, half]
        for n in range(len(probes)):
            at = pl.ds(row_at[n], size)
            inside = lane >= col_at[n]
            t_real = jnp.where(inside, ext[0, 0, at, :], ext[0, 1, at, :])
            t_imag = jnp.where(inside, ext[1, 0, at, :], ext[1, 1, at, :])
            real, imag = state[n, 0], state[n, 1]
            rows = slice(n * size, (n + 1) * size)
            x_high[rows, :size], x_low[rows, :size] = split(real * t_real - imag * t_imag)
            x_high[rows, size:], x_low[rows, size:] = split(real * t_imag + imag * t_real)
        y = (
            product(x_high[...], right_ref[0])
            + product(x_high[...], right_ref[1])
            + product(x_low[...], right_ref[0])
        )
        for n in range(len(probes)):
            rows = slice(n * size, (n + 1) * size)
            r_high[:size, rows], r_low[:size, rows] = split(y[rows, :size])
            r_high[size:, rows], r_low[size:, rows] = split(y[rows, size:])
        z = (
            product(left_ref[0], r_high[...])
            + product(left_ref[1], r_high[...])
            + product(left_ref[0], r_low[...])
        )
        for n in range(len(probes)):
            rows = slice(n * size, (n + 1) * size)
            for part in range(2):
                wave = z[part * size : (part + 1) * size, rows]
                if j == count - 1:
                    if ends:
                        wave = pltpu.roll(wave, (size - col_at[n]) & (size - 1), 1)
                    out_ref[n, part] = wave
                else:
                    state[n, part] = wave
    if with_out:
        copy = pltpu.make_async_copy(
            out_ref, final_ref.at[tick, pl.ds(probes[0], len(probes))], sem
        )
        copy.start()
        copy.wait()


def vmem():
    return pl.BlockSpec(memory_space=pltpu.VMEM)


def section(
    tick, layers, probes, scans, tables, wave, *, pieces=None, exts=None,
    probe_wave=None, out=None, starts, ends, tile_rows, name
):
    size = wave.shape[-1]
    with_rim = pieces is not None
    count = len(layers)
    n = len(probes)
    operands = [*scans, wave]
    specs = [pl.BlockSpec(memory_space=pltpu.SMEM)] * 2
    first = probes[0] if wave.shape[0] != n else 0
    specs.append(pl.BlockSpec((n, 2, size, size), lambda i: (first // n, 0, 0, 0)))
    if probe_wave is not None:
        operands.append(probe_wave)
        specs.append(vmem())
    operands += list(tables)
    specs += [vmem()] * 2
    out_shape = [jax.ShapeDtypeStruct((n, 2, size, size), jnp.float32)]
    out_specs = [vmem()]
    if with_rim:
        operands += [piece for piece, _ in pieces]
        for _, at in pieces:
            specs.append(
                pl.BlockSpec((count, 2, 2, size, size), lambda i, at=at: (at, 0, 0, 0, 0))
            )
        out_shape += [
            jax.ShapeDtypeStruct((2, 2, tile_rows + size, size), jnp.float32)
        ] * count
        out_specs += [vmem()] * count
    else:
        operands += list(exts)
        specs += [vmem()] * count
    aliases = {}
    scratch = []
    if out is not None:
        aliases = {len(operands): 0}
        operands.append(out)
        specs.append(pl.BlockSpec(memory_space=pltpu.HBM))
        out_shape = [jax.ShapeDtypeStruct(out.shape, out.dtype)]
        out_specs = [pl.BlockSpec(memory_space=pltpu.HBM)]
        scratch = [pltpu.SemaphoreType.DMA, pltpu.VMEM((n, 2, size, size), jnp.float32)]
    flops = count * n * 2 * 3 * 2 * size * (2 * size) ** 2
    return pl.pallas_call(
        functools.partial(
            section_kernel, tick, layers, probes, with_rim, starts, ends,
            probe_wave is not None, out is not None, tile_rows,
        ),
        input_output_aliases=aliases,
        grid=(1,),
        in_specs=specs,
        out_specs=out_specs,
        out_shape=out_shape,
        scratch_shapes=[
            pltpu.VMEM((n, 2, size, size), jnp.float32),
            pltpu.VMEM((n * size, 2 * size), jnp.bfloat16),
            pltpu.VMEM((n * size, 2 * size), jnp.bfloat16),
            pltpu.VMEM((2 * size, n * size), jnp.bfloat16),
            pltpu.VMEM((2 * size, n * size), jnp.bfloat16),
            *scratch,
        ],
        compiler_params=pltpu.CompilerParams(vmem_limit_bytes=VMEM_LIMIT),
        cost_estimate=pl.CostEstimate(
            flops=flops, bytes_accessed=count * 2 * 2 * 384 * size * 4, transcendentals=0
        ),
        name=name,
    )(*operands)


def shards(phase_map, absorb, probe_wave, waves_in, scan_rows, scan_cols):
    size = probe_wave.shape[-1]
    slices, tile_rows = phase_map.shape[:2]
    tiles = lax.axis_size("tile")
    depth_count = lax.axis_size("depth")
    back = [(i, (i - 1) % tiles) for i in range(tiles)]
    onward = [(i, (i + 1) % depth_count) for i in range(depth_count)]

    per_rim = slices // RIM_CHUNKS
    spans = [list(range(r * per_rim, (r + 1) * per_rim)) for r in range(RIM_CHUNKS)]
    firsts, rims = [], []
    for r, layers in enumerate(spans):
        firsts.append(trans_rows(phase_map, absorb, size, layers, 0, f"rim{r}"))
        rims.append(lax.ppermute(firsts[-1], "tile", back))
    rest = trans_rows(phase_map, absorb, size, list(range(slices)), 1, "rest")

    tables = [jnp.asarray(table) for table in hop_tables(size)]
    scans = (scan_rows, scan_cols)
    held = waves_in[0]
    count = held.shape[0]
    per_chunk = count // CHUNKS
    groups = [list(range(c * per_chunk, (c + 1) * per_chunk)) for c in range(CHUNKS)]
    exts = []
    done = []
    for r, layers in enumerate(spans):
        pieces = [(firsts[r], 0), (rest, r), (rims[r], 0)]
        common = dict(starts=r == 0, ends=r == RIM_CHUNKS - 1, tile_rows=tile_rows)
        if r < RIM_CHUNKS - 1:
            held, *made = section(
                0, layers, list(range(count)), scans, tables, held, pieces=pieces,
                name=f"enter{r}", **common,
            )
            exts += made
            continue
        for c, group in enumerate(groups):
            sources = dict(pieces=pieces) if c == 0 else dict(exts=exts[-per_rim:])
            left, *made = section(
                0, layers, group, scans, tables, held, name=f"leave{c}", **sources, **common
            )
            exts += made
            done.append(left)

    out = None
    for tick in range(1, TICKS):
        arrived = [lax.ppermute(left, "depth", onward) for left in done]
        out_shape = jax.ShapeDtypeStruct((TICKS, *held.shape), held.dtype)
        out = store(tick - 1, done, out, out_shape)
        done = []
        for c, group in enumerate(groups):
            (left,) = section(
                tick, list(range(slices)), group, scans, tables, arrived[c], exts=exts,
                probe_wave=probe_wave, out=out if tick == TICKS - 1 else None,
                starts=True, ends=True, tile_rows=tile_rows, name=f"tick{tick}_{c}",
            )
            if tick == TICKS - 1:
                out = left
            done.append(left)
    return out[:, None]


def solution(mesh):
    return jax.shard_map(
        shards,
        mesh=mesh,
        in_specs=(
            P("depth", "tile", None),
            P("depth", "tile", None),
            P(),
            P("depth", "tile", None, None, None),
            P(None, "tile"),
            P(None, "tile"),
        ),
        out_specs=P(None, "depth", "tile", None, None, None),
        check_vma=False,
    )
```

```python
import functools
import math

import jax
import jax.numpy as jnp
import ml_dtypes
import numpy as np
from jax import lax
from jax.experimental import pallas as pl
from jax.experimental.pallas import tpu as pltpu
from jax.sharding import PartitionSpec as P

TICKS = 3
CHUNKS = 2
RIM_CHUNKS = 4

fresnel = 0.1
VMEM_LIMIT = 24 * 1024 * 1024

SIN_TERMS = [(-1.0) ** j / math.factorial(2 * j + 1) for j in range(7)]
COS_TERMS = [(-1.0) ** j / math.factorial(2 * j) for j in range(8)]


def hop_tables(size):
    index = np.arange(size)
    frequency = np.where(index < size // 2, index, index - size).astype(np.float64)
    k = np.exp(-1j * fresnel * math.pi * frequency**2 / size)
    lag = np.fft.ifft(k)
    g = lag[(index[:, None] - index[None, :]) % size]
    right = np.block([[g.real, g.imag], [-g.imag, g.real]])
    high = right.astype(ml_dtypes.bfloat16)
    low = (right - high.astype(np.float64)).astype(ml_dtypes.bfloat16)
    right = np.stack([high, low])
    return right, np.ascontiguousarray(right.transpose(0, 2, 1))


def series(z, terms):
    total = jnp.full_like(z, terms[-1])
    for term in terms[-2::-1]:
        total = total * z + term
    return total


def transmission(phase, absorb):
    t = 0.5 * phase
    z = t * t
    s = t * series(z, SIN_TERMS)
    c = series(z, COS_TERMS)
    damping = jnp.exp(-absorb)
    return damping * (1.0 - 2.0 * (s * s)), damping * (2.0 * (s * c))


def split(x):
    high = x.astype(jnp.bfloat16)
    return high, (x - high.astype(jnp.float32)).astype(jnp.bfloat16)


def product(a, b):
    return jnp.dot(a, b, preferred_element_type=jnp.float32)


def trans_kernel(phase_ref, absorb_ref, out_ref):
    size = out_ref.shape[-1]
    step = 32

    def body(i, carry):
        at = pl.ds(pl.multiple_of(i * step, step), step)
        for layer in range(phase_ref.shape[0]):
            for half in range(2):
                cols = slice(half * size, (half + 1) * size)
                real, imag = transmission(phase_ref[layer, at, cols], absorb_ref[layer, at, cols])
                out_ref[layer, 0, half, at, :] = real
                out_ref[layer, 1, half, at, :] = imag
        return carry

    lax.fori_loop(0, phase_ref.shape[1] // step, body, 0)


def first_trans_kernel(phase_ref, absorb_ref, out_ref, phase_buf, absorb_buf, sem):
    copies = []
    for n, (ref, buf) in enumerate([(phase_ref, phase_buf), (absorb_ref, absorb_buf)]):
        source = ref.at[pl.ds(0, buf.shape[0]), pl.ds(0, buf.shape[1])]
        copies.append(pltpu.make_async_copy(source, buf, sem.at[n]))
        copies[-1].start()
    for copy in copies:
        copy.wait()
    trans_kernel(phase_buf, absorb_buf, out_ref)


def trans_rows(phase_map, absorb, size, layers, block, name, direct=False):
    count = len(layers)
    columns = phase_map.shape[2]
    at = layers[0] // count
    spec = pl.BlockSpec((count, size, columns), lambda i: (at, block, 0))
    values = count * size * columns
    kernel, scratch = trans_kernel, []
    if direct:
        kernel = first_trans_kernel
        spec = pl.BlockSpec(memory_space=pltpu.HBM)
        scratch = [pltpu.VMEM((count, size, columns), jnp.float32)] * 2
        scratch.append(pltpu.SemaphoreType.DMA((2,)))
    return pl.pallas_call(
        kernel,
        grid=(1,),
        scratch_shapes=scratch,
        out_shape=jax.ShapeDtypeStruct((count, 2, columns // size, size, size), jnp.float32),
        in_specs=[spec] * 2,
        out_specs=vmem(),
        compiler_params=pltpu.CompilerParams(vmem_limit_bytes=VMEM_LIMIT),
        cost_estimate=pl.CostEstimate(
            flops=values * 40, bytes_accessed=values * 16, transcendentals=values
        ),
        name=name,
    )(phase_map, absorb)


def advance(
    tick, layers, probes, starts, ends, piece_refs, ext_refs, scans, waves, put, tables, scratch
):
    rows_ref, cols_ref, tile_rows = scans
    right_ref, left_ref = tables
    state, x_high, x_low, r_high, r_low = scratch
    size = state.shape[-1]
    batch = tick - lax.axis_index("depth") + lax.axis_size("depth") - 1
    offset = lax.axis_index("tile") * tile_rows
    row_at = [rows_ref[batch, p] - offset for p in probes]
    col_at = [cols_ref[batch, p] for p in probes]
    lane = lax.broadcasted_iota(jnp.int32, (size, size), 1)
    count = len(layers)

    for n in range(len(probes)):
        for part in range(2):
            wave = waves(n, part)
            if starts:
                wave = pltpu.roll(wave, col_at[n] & (size - 1), 1)
            state[n, part] = wave

    for j in range(count):
        ext = ext_refs[j]
        for piece, piece_ref in enumerate(piece_refs):
            rows = slice(piece * size, (piece + 1) * size)
            for part in range(2):
                for half in range(2):
                    ext[part, half, rows, :] = piece_ref[j, part, half]
        for n in range(len(probes)):
            at = pl.ds(row_at[n], size)
            inside = lane >= col_at[n]
            t_real = jnp.where(inside, ext[0, 0, at, :], ext[0, 1, at, :])
            t_imag = jnp.where(inside, ext[1, 0, at, :], ext[1, 1, at, :])
            real, imag = state[n, 0], state[n, 1]
            rows = slice(n * size, (n + 1) * size)
            x_high[rows, :size], x_low[rows, :size] = split(real * t_real - imag * t_imag)
            x_high[rows, size:], x_low[rows, size:] = split(real * t_imag + imag * t_real)
        y = (
            product(x_high[...], right_ref[0])
            + product(x_high[...], right_ref[1])
            + product(x_low[...], right_ref[0])
        )
        for n in range(len(probes)):
            rows = slice(n * size, (n + 1) * size)
            r_high[:size, rows], r_low[:size, rows] = split(y[rows, :size])
            r_high[size:, rows], r_low[size:, rows] = split(y[rows, size:])
        z = (
            product(left_ref[0], r_high[...])
            + product(left_ref[1], r_high[...])
            + product(left_ref[0], r_low[...])
        )
        for n in range(len(probes)):
            rows = slice(n * size, (n + 1) * size)
            for part in range(2):
                wave = z[part * size : (part + 1) * size, rows]
                if j < count - 1:
                    state[n, part] = wave
                    continue
                if ends:
                    wave = pltpu.roll(wave, (size - col_at[n]) & (size - 1), 1)
                put(n, part, wave)


def take(refs, count):
    return [refs.pop(0) for _ in range(count)]


def entry_kernel(layers, probes, with_pieces, starts, ends, tile_rows, *refs):
    refs = list(refs)
    rows_ref, cols_ref, wave_ref, right_ref, left_ref = take(refs, 5)
    if with_pieces:
        piece_refs = take(refs, 3)
        (out_ref,) = take(refs, 1)
        ext_refs = take(refs, len(layers))
    else:
        piece_refs = []
        ext_refs = take(refs, len(layers))
        (out_ref,) = take(refs, 1)

    def put(n, part, wave):
        out_ref[n, part] = wave

    advance(
        0, layers, probes, starts, ends, piece_refs, ext_refs, (rows_ref, cols_ref, tile_rows),
        lambda n, part: wave_ref[n, part], put, (right_ref, left_ref), refs,
    )


def first_kernel(tick, layers, tile_rows, *refs):
    refs = list(refs)
    rows_ref, cols_ref, probe_ref, right_ref, left_ref = take(refs, 5)
    ext_refs = take(refs, len(layers))
    _, out_ref = take(refs, 2)
    count = out_ref.shape[0]
    probes = [pl.program_id(0) * count + n for n in range(count)]

    def put(n, part, wave):
        out_ref[n, part] = wave

    @pl.when(lax.axis_index("depth") == 0)
    def _():
        advance(
            tick, layers, probes, True, True, [], ext_refs, (rows_ref, cols_ref, tile_rows),
            lambda n, part: probe_ref[part], put, (right_ref, left_ref), refs,
        )


def tick_kernel(tick, layers, probes, stores, own_store, tile_rows, *refs):
    refs = list(refs)
    rows_ref, cols_ref, wave_ref, right_ref, left_ref = take(refs, 5)
    ext_refs = take(refs, len(layers))
    (first_ref,) = take(refs, 1)
    stored_refs = take(refs, len(stores))
    if own_store:
        take(refs, 1)
        (final_ref,) = take(refs, 1)
        sem, out_ref = refs.pop(), refs.pop()
    elif stores:
        out_ref, final_ref = take(refs, 2)
        sem = refs.pop()
    else:
        (out_ref,) = take(refs, 1)

    copies = []
    for n, ((to, at), ref) in enumerate(zip(stores, stored_refs)):
        into = final_ref.at[to, pl.ds(at, ref.shape[0])]
        copies.append(pltpu.make_async_copy(ref, into, sem.at[n]))
        copies[-1].start()

    def put(n, part, wave):
        out_ref[n, part] = wave

    depth = lax.axis_index("depth")

    @pl.when(depth == 0)
    def _():
        out_ref[...] = first_ref[...]

    @pl.when(depth != 0)
    def _():
        advance(
            tick, layers, probes, True, True, [], ext_refs, (rows_ref, cols_ref, tile_rows),
            lambda n, part: wave_ref[n, part], put, (right_ref, left_ref), refs,
        )

    if own_store:
        into = final_ref.at[tick, pl.ds(probes[0], len(probes))]
        copies.append(pltpu.make_async_copy(out_ref, into, sem.at[len(stores)]))
        copies[-1].start()
    for copy in copies:
        copy.wait()


def vmem():
    return pl.BlockSpec(memory_space=pltpu.VMEM)


def smem():
    return pl.BlockSpec(memory_space=pltpu.SMEM)


def hbm():
    return pl.BlockSpec(memory_space=pltpu.HBM)


def call(kernel, operands, specs, out_shape, out_specs, n, size, layers, name, **rest):
    grid = rest.pop("grid", (1,))
    flops = grid[0] * layers * n * 2 * 3 * 2 * size * (2 * size) ** 2
    return pl.pallas_call(
        kernel,
        grid=grid,
        in_specs=specs,
        out_specs=out_specs,
        out_shape=out_shape,
        scratch_shapes=[
            pltpu.VMEM((n, 2, size, size), jnp.float32),
            pltpu.VMEM((n * size, 2 * size), jnp.bfloat16),
            pltpu.VMEM((n * size, 2 * size), jnp.bfloat16),
            pltpu.VMEM((2 * size, n * size), jnp.bfloat16),
            pltpu.VMEM((2 * size, n * size), jnp.bfloat16),
            *rest.pop("scratch", []),
        ],
        compiler_params=pltpu.CompilerParams(vmem_limit_bytes=VMEM_LIMIT),
        cost_estimate=pl.CostEstimate(
            flops=flops, bytes_accessed=layers * 2 * 2 * 384 * size * 4, transcendentals=0
        ),
        name=name,
        **rest,
    )(*operands)


def entry(layers, probes, scans, tables, wave, pieces, exts, starts, ends, tile_rows, name):
    size = wave.shape[-1]
    count, n = len(layers), len(probes)
    first = probes[0] // n if wave.shape[0] != n else 0
    operands = [*scans, wave, *tables]
    specs = [
        smem(), smem(), pl.BlockSpec((n, 2, size, size), lambda i: (first, 0, 0, 0)),
        vmem(), vmem(),
    ]
    out_shape = [jax.ShapeDtypeStruct((n, 2, size, size), jnp.float32)]
    if pieces is not None:
        operands += [piece for piece, _ in pieces]
        for _, at in pieces:
            specs.append(
                pl.BlockSpec((count, 2, 2, size, size), lambda i, at=at: (at, 0, 0, 0, 0))
            )
        out_shape += [
            jax.ShapeDtypeStruct((2, 2, tile_rows + size, size), jnp.float32)
        ] * count
    else:
        operands += exts
        specs += [vmem()] * count
    kernel = functools.partial(
        entry_kernel, layers, probes, pieces is not None, starts, ends, tile_rows
    )
    return call(
        kernel, operands, specs, out_shape, [vmem()] * len(out_shape), n, size, count, name
    )


def first_section(tick, n, scans, tables, probe_wave, exts, after, tile_rows, chunks):
    size = probe_wave.shape[-1]
    layers = list(range(len(exts)))
    return call(
        functools.partial(first_kernel, tick, layers, tile_rows),
        [*scans, probe_wave, *tables, *exts, after],
        [smem()] * 2 + [vmem()] * (3 + len(exts)) + [pl.BlockSpec(memory_space=pl.ANY)],
        jax.ShapeDtypeStruct((chunks * n, 2, size, size), jnp.float32),
        pl.BlockSpec((n, 2, size, size), lambda i: (i, 0, 0, 0)),
        n, size, len(exts), f"first{tick}", grid=(chunks,),
    )


def tick_section(
    tick, c, n, scans, tables, wave, exts, first, tile_rows, stored=(), out_shape=None, out=None
):
    size = wave.shape[-1]
    count = len(exts)
    probes = list(range(c * n, (c + 1) * n))
    operands = [*scans, wave, *tables, *exts, first, *(part for _, part in stored)]
    specs = [smem()] * 2 + [vmem()] * (3 + count)
    specs.append(pl.BlockSpec((n, 2, size, size), lambda i: (c, 0, 0, 0)))
    specs += [vmem()] * len(stored)
    shape = [jax.ShapeDtypeStruct((n, 2, size, size), jnp.float32)]
    out_specs = [vmem()]
    rest = {}
    if out is not None:
        rest["input_output_aliases"] = {len(operands): 0}
        operands.append(out)
        specs.append(hbm())
        shape, out_specs = [jax.ShapeDtypeStruct(out.shape, out.dtype)], [hbm()]
        rest["scratch"] = [
            pltpu.VMEM((n, 2, size, size), jnp.float32),
            pltpu.SemaphoreType.DMA((len(stored) + 1,)),
        ]
    elif stored:
        shape.append(out_shape)
        out_specs.append(hbm())
        rest["scratch"] = [pltpu.SemaphoreType.DMA((len(stored),))]
    kernel = functools.partial(
        tick_kernel, tick, list(range(count)), probes, [to for to, _ in stored],
        out is not None, tile_rows,
    )
    return call(
        kernel, operands, specs, shape, out_specs, n, size, count, f"tick{tick}_{c}", **rest
    )


def shards(phase_map, absorb, probe_wave, waves_in, scan_rows, scan_cols):
    size = probe_wave.shape[-1]
    slices, tile_rows = phase_map.shape[:2]
    tiles = lax.axis_size("tile")
    depth_count = lax.axis_size("depth")
    back = [(i, (i - 1) % tiles) for i in range(tiles)]
    onward = [(i, (i + 1) % depth_count) for i in range(depth_count)]

    per_rim = slices // RIM_CHUNKS
    spans = [list(range(r * per_rim, (r + 1) * per_rim)) for r in range(RIM_CHUNKS)]
    firsts, rims = [], []
    for r, layers in enumerate(spans):
        firsts.append(trans_rows(phase_map, absorb, size, layers, 0, f"rim{r}", r == 0))
        rims.append(lax.ppermute(firsts[-1], "tile", back))
    rest = trans_rows(phase_map, absorb, size, list(range(slices)), 1, "rest")

    tables = [jnp.asarray(table) for table in hop_tables(size)]
    scans = (scan_rows, scan_cols)
    held = waves_in[0]
    count = held.shape[0]
    per_chunk = count // CHUNKS
    groups = [list(range(c * per_chunk, (c + 1) * per_chunk)) for c in range(CHUNKS)]
    exts = []
    done = []
    for r, layers in enumerate(spans):
        pieces = [(firsts[r], 0), (rest, r), (rims[r], 0)]
        edges = (r == 0, r == RIM_CHUNKS - 1, tile_rows)
        if r < RIM_CHUNKS - 1:
            held, *made = entry(
                layers, list(range(count)), scans, tables, held, pieces, None, *edges, f"enter{r}"
            )
            exts += made
            continue
        for c, group in enumerate(groups):
            sources = (pieces, None) if c == 0 else (None, exts[-per_rim:])
            left, *made = entry(
                layers, group, scans, tables, held, *sources, *edges, f"leave{c}"
            )
            exts += made
            done.append(left)

    stored = []
    for tick in range(1, TICKS):
        stored += [((tick - 1, c * per_chunk), part) for c, part in enumerate(done)]
        arrived = [lax.ppermute(left, "depth", onward) for left in done]
        first = first_section(
            tick, per_chunk, scans, tables, probe_wave, exts, done[-1], tile_rows, CHUNKS
        )
        done = []
        out = None
        for c in range(CHUNKS):
            last = {}
            if tick == TICKS - 1:
                shape = jax.ShapeDtypeStruct((TICKS, count, *held.shape[1:]), held.dtype)
                last = dict(stored=stored, out_shape=shape)
                if c == CHUNKS - 1:
                    last = dict(stored=stored, out=out)
            left, *made = tick_section(
                tick, c, per_chunk, scans, tables, arrived[c], exts, first, tile_rows, **last
            )
            if made:
                out = made[0]
                stored = [((tick, c * per_chunk), left)]
            done.append(left)
    out = done[-1]
    return out[:, None]


def solution(mesh):
    return jax.shard_map(
        shards,
        mesh=mesh,
        in_specs=(
            P("depth", "tile", None),
            P("depth", "tile", None),
            P(),
            P("depth", "tile", None, None, None),
            P(None, "tile"),
            P(None, "tile"),
        ),
        out_specs=P(None, "depth", "tile", None, None, None),
        check_vma=False,
    )
```

```python
import functools
import math

import jax
import jax.numpy as jnp
import ml_dtypes
import numpy as np
from jax import lax
from jax.experimental import pallas as pl
from jax.experimental.pallas import tpu as pltpu
from jax.sharding import PartitionSpec as P

TICKS = 3
CHUNKS = 2

fresnel = 0.1
VMEM_LIMIT = 24 * 1024 * 1024
WIDE_LIMIT = 62 * 1024 * 1024

SIN_TERMS = [(-1.0) ** j / math.factorial(2 * j + 1) for j in range(7)]
COS_TERMS = [(-1.0) ** j / math.factorial(2 * j) for j in range(8)]


def hop_tables(size):
    index = np.arange(size)
    frequency = np.where(index < size // 2, index, index - size).astype(np.float64)
    k = np.exp(-1j * fresnel * math.pi * frequency**2 / size)
    lag = np.fft.ifft(k)
    g = lag[(index[:, None] - index[None, :]) % size]
    right = np.block([[g.real, g.imag], [-g.imag, g.real]])
    high = right.astype(ml_dtypes.bfloat16)
    low = (right - high.astype(np.float64)).astype(ml_dtypes.bfloat16)
    right = np.stack([high, low])
    return right, np.ascontiguousarray(right.transpose(0, 2, 1))


def series(z, terms):
    total = jnp.full_like(z, terms[-1])
    for term in terms[-2::-1]:
        total = total * z + term
    return total


def transmission(phase, absorb):
    t = 0.5 * phase
    z = t * t
    s = t * series(z, SIN_TERMS)
    c = series(z, COS_TERMS)
    damping = jnp.exp(-absorb)
    return damping * (1.0 - 2.0 * (s * s)), damping * (2.0 * (s * c))


def split(x):
    high = x.astype(jnp.bfloat16)
    return high, (x - high.astype(jnp.float32)).astype(jnp.bfloat16)


def product(a, b):
    return jnp.dot(a, b, preferred_element_type=jnp.float32)


def trans_layer(phase_ref, absorb_ref, out_ref):
    rows, columns = phase_ref.shape
    size = out_ref.shape[-1]
    step = 32

    def body(i, carry):
        at = pl.ds(pl.multiple_of(i * step, step), step)
        for half in range(columns // size):
            cols = slice(half * size, (half + 1) * size)
            real, imag = transmission(phase_ref[at, cols], absorb_ref[at, cols])
            out_ref[0, half, at, :] = real
            out_ref[1, half, at, :] = imag
        return carry

    lax.fori_loop(0, rows // step, body, 0)


def edge_kernel(phase_ref, absorb_ref, *refs):
    *out_refs, phase_buf, absorb_buf, sem = refs
    count, rows = phase_buf.shape[:2]
    copies = []
    for layer in range(count):
        for n, (ref, buf) in enumerate([(phase_ref, phase_buf), (absorb_ref, absorb_buf)]):
            source = ref.at[layer, pl.ds(0, rows)]
            copies.append(pltpu.make_async_copy(source, buf.at[layer], sem.at[2 * layer + n]))
            copies[-1].start()
    for layer in range(count):
        copies[2 * layer].wait()
        copies[2 * layer + 1].wait()
        trans_layer(phase_buf.at[layer], absorb_buf.at[layer], out_refs[layer].at[0])


def rest_kernel(phase_ref, absorb_ref, out_ref):
    for layer in range(phase_ref.shape[0]):
        trans_layer(phase_ref.at[layer], absorb_ref.at[layer], out_ref.at[layer])


def edge_rows(phase_map, absorb, size):
    count, _, columns = phase_map.shape
    shape = jax.ShapeDtypeStruct((1, 2, columns // size, size, size), jnp.float32)
    values = count * size * columns
    return pl.pallas_call(
        edge_kernel,
        out_shape=[shape] * count,
        in_specs=[hbm()] * 2,
        out_specs=[vmem()] * count,
        scratch_shapes=[
            pltpu.VMEM((count, size, columns), jnp.float32),
            pltpu.VMEM((count, size, columns), jnp.float32),
            pltpu.SemaphoreType.DMA((2 * count,)),
        ],
        compiler_params=pltpu.CompilerParams(vmem_limit_bytes=WIDE_LIMIT),
        cost_estimate=pl.CostEstimate(
            flops=values * 40, bytes_accessed=values * 16, transcendentals=values
        ),
        name="edge",
    )(phase_map, absorb)


def rest_rows(phase_map, absorb, size):
    count, rows, columns = phase_map.shape
    spec = pl.BlockSpec((count, rows - size, columns), lambda i: (0, 1, 0))
    values = count * (rows - size) * columns
    return pl.pallas_call(
        rest_kernel,
        grid=(1,),
        out_shape=jax.ShapeDtypeStruct((count, 2, columns // size, rows - size, size), jnp.float32),
        in_specs=[spec] * 2,
        out_specs=vmem(),
        compiler_params=pltpu.CompilerParams(vmem_limit_bytes=VMEM_LIMIT),
        cost_estimate=pl.CostEstimate(
            flops=values * 40, bytes_accessed=values * 16, transcendentals=values
        ),
        name="rest",
    )(phase_map, absorb)


def advance(
    tick, layers, probes, starts, ends, piece_refs, ext_refs, anchors_ref, waves, put, tables, scratch
):
    right_ref, left_ref = tables
    state, x_high, x_low, r_high, r_low = scratch
    size = state.shape[-1]
    each = anchors_ref.shape[0] // (2 * TICKS)
    row_at, col_at = [
        [anchors_ref[pl.ds((2 * tick + axis) * each + p, 1), :][0, 0] for p in probes]
        for axis in range(2)
    ]
    lane = lax.broadcasted_iota(jnp.int32, (size, size), 1)
    count = len(layers)

    for n in range(len(probes)):
        for part in range(2):
            wave = waves(n, part)
            if starts:
                wave = pltpu.roll(wave, col_at[n] & (size - 1), 1)
            state[n, part] = wave

    for j in range(count):
        ext = ext_refs[j]
        for piece, piece_ref in enumerate(piece_refs):
            rows = slice(piece * size, (piece + 1) * size)
            for part in range(2):
                for half in range(2):
                    ext[part, half, rows, :] = piece_ref[j, part, half]
        for n in range(len(probes)):
            at = pl.ds(row_at[n], size)
            inside = lane >= col_at[n]
            t_real = jnp.where(inside, ext[0, 0, at, :], ext[0, 1, at, :])
            t_imag = jnp.where(inside, ext[1, 0, at, :], ext[1, 1, at, :])
            real, imag = state[n, 0], state[n, 1]
            rows = slice(n * size, (n + 1) * size)
            x_high[rows, :size], x_low[rows, :size] = split(real * t_real - imag * t_imag)
            x_high[rows, size:], x_low[rows, size:] = split(real * t_imag + imag * t_real)
        y = (
            product(x_high[...], right_ref[0])
            + product(x_high[...], right_ref[1])
            + product(x_low[...], right_ref[0])
        )
        for n in range(len(probes)):
            rows = slice(n * size, (n + 1) * size)
            r_high[:size, rows], r_low[:size, rows] = split(y[rows, :size])
            r_high[size:, rows], r_low[size:, rows] = split(y[rows, size:])
        z = (
            product(left_ref[0], r_high[...])
            + product(left_ref[1], r_high[...])
            + product(left_ref[0], r_low[...])
        )
        for n in range(len(probes)):
            rows = slice(n * size, (n + 1) * size)
            for part in range(2):
                wave = z[part * size : (part + 1) * size, rows]
                if j < count - 1:
                    state[n, part] = wave
                    continue
                if ends:
                    wave = pltpu.roll(wave, (size - col_at[n]) & (size - 1), 1)
                put(n, part, wave)


def take(refs, count):
    return [refs.pop(0) for _ in range(count)]


def entry_kernel(layers, probes, with_pieces, starts, ends, *refs):
    refs = list(refs)
    anchors_ref, wave_ref, right_ref, left_ref = take(refs, 4)
    if with_pieces:
        piece_refs = take(refs, 3)
        (out_ref,) = take(refs, 1)
        ext_refs = take(refs, len(layers))
    else:
        piece_refs = []
        ext_refs = take(refs, len(layers))
        (out_ref,) = take(refs, 1)

    def put(n, part, wave):
        out_ref[n, part] = wave

    advance(
        0, layers, probes, starts, ends, piece_refs, ext_refs, anchors_ref,
        lambda n, part: wave_ref[n, part], put, (right_ref, left_ref), refs,
    )


def first_kernel(tick, layers, *refs):
    refs = list(refs)
    anchors_ref, probe_ref, right_ref, left_ref = take(refs, 4)
    ext_refs = take(refs, len(layers))
    _, out_ref = take(refs, 2)
    count = out_ref.shape[0]
    probes = [pl.program_id(0) * count + n for n in range(count)]

    def put(n, part, wave):
        out_ref[n, part] = wave

    @pl.when(lax.axis_index("depth") == 0)
    def _():
        advance(
            tick, layers, probes, True, True, [], ext_refs, anchors_ref,
            lambda n, part: probe_ref[part], put, (right_ref, left_ref), refs,
        )


def tick_kernel(tick, layers, probes, stores, own_store, *refs):
    refs = list(refs)
    anchors_ref, wave_ref, right_ref, left_ref = take(refs, 4)
    ext_refs = take(refs, len(layers))
    (first_ref,) = take(refs, 1)
    stored_refs = take(refs, len(stores))
    if own_store:
        take(refs, 1)
        (final_ref,) = take(refs, 1)
        sem, out_ref = refs.pop(), refs.pop()
    elif stores:
        out_ref, final_ref = take(refs, 2)
        sem = refs.pop()
    else:
        (out_ref,) = take(refs, 1)

    copies = []
    for n, ((to, at), ref) in enumerate(zip(stores, stored_refs)):
        into = final_ref.at[to, pl.ds(at, ref.shape[0])]
        copies.append(pltpu.make_async_copy(ref, into, sem.at[n]))
        copies[-1].start()

    def put(n, part, wave):
        out_ref[n, part] = wave

    depth = lax.axis_index("depth")

    @pl.when(depth == 0)
    def _():
        out_ref[...] = first_ref[...]

    @pl.when(depth != 0)
    def _():
        advance(
            tick, layers, probes, True, True, [], ext_refs, anchors_ref,
            lambda n, part: wave_ref[n, part], put, (right_ref, left_ref), refs,
        )

    if own_store:
        into = final_ref.at[tick, pl.ds(probes[0], len(probes))]
        copies.append(pltpu.make_async_copy(out_ref, into, sem.at[len(stores)]))
        copies[-1].start()
    for copy in copies:
        copy.wait()


def vmem():
    return pl.BlockSpec(memory_space=pltpu.VMEM)


def hbm():
    return pl.BlockSpec(memory_space=pltpu.HBM)


def call(kernel, operands, specs, out_shape, out_specs, n, size, layers, name, **rest):
    grid = rest.pop("grid", (1,))
    flops = grid[0] * layers * n * 2 * 3 * 2 * size * (2 * size) ** 2
    return pl.pallas_call(
        kernel,
        grid=grid,
        in_specs=specs,
        out_specs=out_specs,
        out_shape=out_shape,
        scratch_shapes=[
            pltpu.VMEM((n, 2, size, size), jnp.float32),
            pltpu.VMEM((n * size, 2 * size), jnp.bfloat16),
            pltpu.VMEM((n * size, 2 * size), jnp.bfloat16),
            pltpu.VMEM((2 * size, n * size), jnp.bfloat16),
            pltpu.VMEM((2 * size, n * size), jnp.bfloat16),
            *rest.pop("scratch", []),
        ],
        compiler_params=pltpu.CompilerParams(vmem_limit_bytes=VMEM_LIMIT),
        cost_estimate=pl.CostEstimate(
            flops=flops, bytes_accessed=layers * 2 * 2 * 384 * size * 4, transcendentals=0
        ),
        name=name,
        **rest,
    )(*operands)


def entry(layers, probes, anchors, tables, wave, pieces, exts, starts, ends, tile_rows, name):
    size = wave.shape[-1]
    count, n = len(layers), len(probes)
    first = probes[0] // n if wave.shape[0] != n else 0
    operands = [anchors, wave, *tables]
    specs = [
        vmem(), pl.BlockSpec((n, 2, size, size), lambda i: (first, 0, 0, 0)),
        vmem(), vmem(),
    ]
    out_shape = [jax.ShapeDtypeStruct((n, 2, size, size), jnp.float32)]
    if pieces is not None:
        operands += [piece for piece, _ in pieces]
        for _, at in pieces:
            specs.append(
                pl.BlockSpec((count, 2, 2, size, size), lambda i, at=at: (at, 0, 0, 0, 0))
            )
        out_shape += [
            jax.ShapeDtypeStruct((2, 2, tile_rows + size, size), jnp.float32)
        ] * count
    else:
        operands += exts
        specs += [vmem()] * count
    kernel = functools.partial(
        entry_kernel, layers, probes, pieces is not None, starts, ends
    )
    return call(
        kernel, operands, specs, out_shape, [vmem()] * len(out_shape), n, size, count, name
    )


def first_section(tick, n, anchors, tables, probe_wave, exts, after, chunks):
    size = probe_wave.shape[-1]
    layers = list(range(len(exts)))
    return call(
        functools.partial(first_kernel, tick, layers),
        [anchors, probe_wave, *tables, *exts, after],
        [vmem()] * (4 + len(exts)) + [pl.BlockSpec(memory_space=pl.ANY)],
        jax.ShapeDtypeStruct((chunks * n, 2, size, size), jnp.float32),
        pl.BlockSpec((n, 2, size, size), lambda i: (i, 0, 0, 0)),
        n, size, len(exts), f"first{tick}", grid=(chunks,),
    )


def tick_section(
    tick, c, n, anchors, tables, wave, exts, first, stored=(), out_shape=None, out=None
):
    size = wave.shape[-1]
    count = len(exts)
    probes = list(range(c * n, (c + 1) * n))
    operands = [anchors, wave, *tables, *exts, first, *(part for _, part in stored)]
    specs = [vmem()] * (4 + count)
    specs.append(pl.BlockSpec((n, 2, size, size), lambda i: (c, 0, 0, 0)))
    specs += [vmem()] * len(stored)
    shape = [jax.ShapeDtypeStruct((n, 2, size, size), jnp.float32)]
    out_specs = [vmem()]
    rest = {}
    if out is not None:
        rest["input_output_aliases"] = {len(operands): 0}
        operands.append(out)
        specs.append(hbm())
        shape, out_specs = [jax.ShapeDtypeStruct(out.shape, out.dtype)], [hbm()]
        rest["scratch"] = [
            pltpu.VMEM((n, 2, size, size), jnp.float32),
            pltpu.SemaphoreType.DMA((len(stored) + 1,)),
        ]
    elif stored:
        shape.append(out_shape)
        out_specs.append(hbm())
        rest["scratch"] = [pltpu.SemaphoreType.DMA((len(stored),))]
    kernel = functools.partial(
        tick_kernel, tick, list(range(count)), probes, [to for to, _ in stored],
        out is not None,
    )
    return call(
        kernel, operands, specs, shape, out_specs, n, size, count, f"tick{tick}_{c}", **rest
    )


def shards(phase_map, absorb, probe_wave, waves_in, scan_rows, scan_cols):
    size = probe_wave.shape[-1]
    slices, tile_rows = phase_map.shape[:2]
    tiles = lax.axis_size("tile")
    depth_count = lax.axis_size("depth")
    back = [(i, (i - 1) % tiles) for i in range(tiles)]
    onward = [(i, (i + 1) % depth_count) for i in range(depth_count)]

    firsts = edge_rows(phase_map, absorb, size)
    rims = [lax.ppermute(first, "tile", back) for first in firsts]
    rest = rest_rows(phase_map, absorb, size)

    tables = [jnp.asarray(table) for table in hop_tables(size)]
    depth, tile = lax.axis_index("depth"), lax.axis_index("tile")
    anchors = jnp.stack([scan_rows - tile * tile_rows, scan_cols], 1)
    anchors = lax.dynamic_slice_in_dim(anchors, depth_count - 1 - depth, TICKS, 0)
    anchors = jnp.broadcast_to(anchors.reshape(-1, 1), (anchors.size, size))
    held = waves_in[0]
    count = held.shape[0]
    per_chunk = count // CHUNKS
    groups = [list(range(c * per_chunk, (c + 1) * per_chunk)) for c in range(CHUNKS)]
    exts = []
    done = []
    for r in range(slices):
        layers = [r]
        pieces = [(firsts[r], 0), (rest, r), (rims[r], 0)]
        edges = (r == 0, r == slices - 1, tile_rows)
        if r < slices - 1:
            held, *made = entry(
                layers, list(range(count)), anchors, tables, held, pieces, None, *edges, f"enter{r}"
            )
            exts += made
            continue
        for c, group in enumerate(groups):
            sources = (pieces, None) if c == 0 else (None, exts[-1:])
            left, *made = entry(
                layers, group, anchors, tables, held, *sources, *edges, f"leave{c}"
            )
            exts += made
            done.append(left)

    stored = []
    for tick in range(1, TICKS):
        stored += [((tick - 1, c * per_chunk), part) for c, part in enumerate(done)]
        arrived = [lax.ppermute(left, "depth", onward) for left in done]
        first = first_section(
            tick, per_chunk, anchors, tables, probe_wave, exts, done[-1], CHUNKS
        )
        done = []
        out = None
        for c in range(CHUNKS):
            last = {}
            if tick == TICKS - 1:
                shape = jax.ShapeDtypeStruct((TICKS, count, *held.shape[1:]), held.dtype)
                last = dict(stored=stored, out_shape=shape)
                if c == CHUNKS - 1:
                    last = dict(stored=stored, out=out)
            left, *made = tick_section(
                tick, c, per_chunk, anchors, tables, arrived[c], exts, first, **last
            )
            if made:
                out = made[0]
                stored = [((tick, c * per_chunk), left)]
            done.append(left)
    out = done[-1]
    return out[:, None]


def solution(mesh):
    return jax.shard_map(
        shards,
        mesh=mesh,
        in_specs=(
            P("depth", "tile", None),
            P("depth", "tile", None),
            P(),
            P("depth", "tile", None, None, None),
            P(None, "tile"),
            P(None, "tile"),
        ),
        out_specs=P(None, "depth", "tile", None, None, None),
        check_vma=False,
    )
```

```python
import functools
import math

import jax
import jax.numpy as jnp
import ml_dtypes
import numpy as np
from jax import lax
from jax.experimental import pallas as pl
from jax.experimental.pallas import tpu as pltpu
from jax.sharding import PartitionSpec as P

TICKS = 3
GROUPS = [[0], [1], [2], [3]]

fresnel = 0.1
VMEM_LIMIT = 24 * 1024 * 1024
WEIGHT = 8
WIDE_LIMIT = 62 * 1024 * 1024

SIN_TERMS = [(-1.0) ** j / math.factorial(2 * j + 1) for j in range(7)]
COS_TERMS = [(-1.0) ** j / math.factorial(2 * j) for j in range(8)]


def hop_tables(size):
    index = np.arange(size)
    frequency = np.where(index < size // 2, index, index - size).astype(np.float64)
    k = np.exp(-1j * fresnel * math.pi * frequency**2 / size)
    lag = np.fft.ifft(k)
    g = lag[(index[:, None] - index[None, :]) % size]
    right = np.block([[g.real, g.imag], [-g.imag, g.real]])
    high = right.astype(ml_dtypes.bfloat16)
    low = (right - high.astype(np.float64)).astype(ml_dtypes.bfloat16)
    right = np.stack([high, low])
    return right, np.ascontiguousarray(right.transpose(0, 2, 1))


def series(z, terms):
    total = jnp.full_like(z, terms[-1])
    for term in terms[-2::-1]:
        total = total * z + term
    return total


def transmission(phase, absorb):
    t = 0.5 * phase
    z = t * t
    s = t * series(z, SIN_TERMS)
    c = series(z, COS_TERMS)
    damping = jnp.exp(-absorb)
    return damping * (1.0 - 2.0 * (s * s)), damping * (2.0 * (s * c))


def split(x):
    high = x.astype(jnp.bfloat16)
    return high, (x - high.astype(jnp.float32)).astype(jnp.bfloat16)


def product(a, b):
    return jnp.dot(a, b, preferred_element_type=jnp.float32)


def trans_layer(phase_ref, absorb_ref, out_ref):
    rows, columns = phase_ref.shape
    size = out_ref.shape[-1]
    step = 32

    def body(i, carry):
        at = pl.ds(pl.multiple_of(i * step, step), step)
        for half in range(columns // size):
            cols = slice(half * size, (half + 1) * size)
            real, imag = transmission(phase_ref[at, cols], absorb_ref[at, cols])
            out_ref[0, half, at, :] = real
            out_ref[1, half, at, :] = imag
        return carry

    lax.fori_loop(0, rows // step, body, 0)


def edge_kernel(phase_ref, absorb_ref, *refs):
    *out_refs, phase_buf, absorb_buf, sem = refs
    count, rows = phase_buf.shape[:2]
    copies = []
    for layer in range(count):
        for n, (ref, buf) in enumerate([(phase_ref, phase_buf), (absorb_ref, absorb_buf)]):
            source = ref.at[layer, pl.ds(0, rows)]
            copies.append(pltpu.make_async_copy(source, buf.at[layer], sem.at[2 * layer + n]))
            copies[-1].start()
    for layer in range(count):
        copies[2 * layer].wait()
        copies[2 * layer + 1].wait()
        trans_layer(phase_buf.at[layer], absorb_buf.at[layer], out_refs[layer].at[0])


def rest_kernel(phase_ref, absorb_ref, out_ref):
    for layer in range(phase_ref.shape[0]):
        trans_layer(phase_ref.at[layer], absorb_ref.at[layer], out_ref.at[layer])


def edge_rows(phase_map, absorb, size):
    count, _, columns = phase_map.shape
    shape = jax.ShapeDtypeStruct((1, 2, columns // size, size, size), jnp.float32)
    values = count * size * columns
    return pl.pallas_call(
        edge_kernel,
        out_shape=[shape] * count,
        in_specs=[hbm()] * 2,
        out_specs=[vmem()] * count,
        scratch_shapes=[
            pltpu.VMEM((count, size, columns), jnp.float32),
            pltpu.VMEM((count, size, columns), jnp.float32),
            pltpu.SemaphoreType.DMA((2 * count,)),
        ],
        compiler_params=pltpu.CompilerParams(vmem_limit_bytes=WIDE_LIMIT),
        cost_estimate=pl.CostEstimate(
            flops=values * 40, bytes_accessed=values * 16, transcendentals=values
        ),
        name="edge",
    )(phase_map, absorb)


def rest_rows(phase_map, absorb, size):
    count, rows, columns = phase_map.shape
    spec = pl.BlockSpec((count, rows - size, columns), lambda i: (0, 1, 0))
    values = count * (rows - size) * columns
    return pl.pallas_call(
        rest_kernel,
        grid=(1,),
        out_shape=jax.ShapeDtypeStruct((count, 2, columns // size, rows - size, size), jnp.float32),
        in_specs=[spec] * 2,
        out_specs=vmem(),
        compiler_params=pltpu.CompilerParams(vmem_limit_bytes=VMEM_LIMIT),
        cost_estimate=pl.CostEstimate(
            flops=values * 40, bytes_accessed=values * 16, transcendentals=values
        ),
        name="rest",
    )(phase_map, absorb)


def advance(
    tick, layers, probes, starts, ends, piece_refs, ext_refs, anchors_ref, waves, put, tables, scratch
):
    right_ref, left_ref = tables
    state, x_high, x_low, r_high, r_low = scratch
    size = state.shape[-1]
    each = anchors_ref.shape[0] // (2 * TICKS)
    row_at, col_at = [
        [anchors_ref[pl.ds((2 * tick + axis) * each + p, 1), :][0, 0] for p in probes]
        for axis in range(2)
    ]
    lane = lax.broadcasted_iota(jnp.int32, (size, size), 1)
    count = len(layers)

    for n in range(len(probes)):
        for part in range(2):
            wave = waves(n, part)
            if starts:
                wave = pltpu.roll(wave, col_at[n] & (size - 1), 1)
            state[n, part] = wave

    for j in range(count):
        ext = ext_refs[j]
        for piece, piece_ref in enumerate(piece_refs):
            rows = slice(piece * size, (piece + 1) * size)
            for part in range(2):
                for half in range(2):
                    ext[part, half, rows, :] = piece_ref[j, part, half]
        for n in range(len(probes)):
            at = pl.ds(row_at[n], size)
            inside = lane >= col_at[n]
            t_real = jnp.where(inside, ext[0, 0, at, :], ext[0, 1, at, :])
            t_imag = jnp.where(inside, ext[1, 0, at, :], ext[1, 1, at, :])
            real, imag = state[n, 0], state[n, 1]
            rows = slice(n * size, (n + 1) * size)
            x_high[rows, :size], x_low[rows, :size] = split(real * t_real - imag * t_imag)
            x_high[rows, size:], x_low[rows, size:] = split(real * t_imag + imag * t_real)
        y = (
            product(x_high[...], right_ref[0])
            + product(x_high[...], right_ref[1])
            + product(x_low[...], right_ref[0])
        )
        for n in range(len(probes)):
            rows = slice(n * size, (n + 1) * size)
            r_high[:size, rows], r_low[:size, rows] = split(y[rows, :size])
            r_high[size:, rows], r_low[size:, rows] = split(y[rows, size:])
        z = (
            product(left_ref[0], r_high[...])
            + product(left_ref[1], r_high[...])
            + product(left_ref[0], r_low[...])
        )
        for n in range(len(probes)):
            rows = slice(n * size, (n + 1) * size)
            for part in range(2):
                wave = z[part * size : (part + 1) * size, rows]
                if j < count - 1:
                    state[n, part] = wave
                    continue
                if ends:
                    wave = pltpu.roll(wave, (size - col_at[n]) & (size - 1), 1)
                put(n, part, wave)


def take(refs, count):
    return [refs.pop(0) for _ in range(count)]


def entry_kernel(layers, groups, base, with_pieces, starts, ends, with_after, *refs):
    refs = list(refs)
    anchors_ref, wave_ref, right_ref, left_ref = take(refs, 4)
    if with_pieces:
        piece_refs = take(refs, 3)
        take(refs, with_after)
        out_refs = take(refs, len(groups))
        ext_refs = take(refs, len(layers))
    else:
        piece_refs = []
        ext_refs = take(refs, len(layers))
        take(refs, with_after)
        out_refs = take(refs, len(groups))
    places = [(g, at) for g, group in enumerate(groups) for at in range(len(group))]

    def put(n, part, wave):
        g, at = places[n]
        out_refs[g][at, part] = wave

    advance(
        0, layers, sum(groups, []), starts, ends, piece_refs, ext_refs, anchors_ref,
        lambda n, part: wave_ref[base + n, part], put, (right_ref, left_ref), refs,
    )


def first_kernel(tick, layers, *refs):
    refs = list(refs)
    anchors_ref, probe_ref, right_ref, left_ref = take(refs, 4)
    ext_refs = take(refs, len(layers))
    _, out_ref = take(refs, 2)
    count = out_ref.shape[0]
    probes = [pl.program_id(0) * count + n for n in range(count)]

    def put(n, part, wave):
        out_ref[n, part] = wave

    @pl.when(lax.axis_index("depth") == 0)
    def _():
        advance(
            tick, layers, probes, True, True, [], ext_refs, anchors_ref,
            lambda n, part: probe_ref[part], put, (right_ref, left_ref), refs,
        )


def tick_kernel(tick, layers, probes, stores, own_store, with_after, *refs):
    refs = list(refs)
    anchors_ref, wave_ref, right_ref, left_ref = take(refs, 4)
    ext_refs = take(refs, len(layers))
    (first_ref,) = take(refs, 1)
    stored_refs = take(refs, len(stores))
    if own_store:
        take(refs, 1 + with_after)
        (final_ref,) = take(refs, 1)
        sem, out_ref = refs.pop(), refs.pop()
    elif stores:
        take(refs, with_after)
        out_ref, final_ref = take(refs, 2)
        sem = refs.pop()
    else:
        take(refs, with_after)
        (out_ref,) = take(refs, 1)

    copies = []
    for n, ((to, at), ref) in enumerate(zip(stores, stored_refs)):
        into = final_ref.at[to, pl.ds(at, ref.shape[0])]
        copies.append(pltpu.make_async_copy(ref, into, sem.at[n]))
        copies[-1].start()

    def put(n, part, wave):
        out_ref[n, part] = wave

    depth = lax.axis_index("depth")

    @pl.when(depth == 0)
    def _():
        out_ref[...] = first_ref[probes[0] : probes[0] + len(probes)]

    @pl.when(depth != 0)
    def _():
        advance(
            tick, layers, probes, True, True, [], ext_refs, anchors_ref,
            lambda n, part: wave_ref[n, part], put, (right_ref, left_ref), refs,
        )

    if own_store:
        into = final_ref.at[tick, pl.ds(probes[0], len(probes))]
        copies.append(pltpu.make_async_copy(out_ref, into, sem.at[len(stores)]))
        copies[-1].start()
    for copy in copies:
        copy.wait()


def vmem():
    return pl.BlockSpec(memory_space=pltpu.VMEM)


def hbm():
    return pl.BlockSpec(memory_space=pltpu.HBM)


def call(kernel, operands, specs, out_shape, out_specs, n, size, layers, name, **rest):
    grid = rest.pop("grid", (1,))
    flops = WEIGHT * grid[0] * layers * n * 2 * 3 * 2 * size * (2 * size) ** 2
    after = rest.pop("after", None)
    if after is not None:
        operands.append(after)
        specs.append(pl.BlockSpec(memory_space=pl.ANY))
    return pl.pallas_call(
        kernel,
        grid=grid,
        in_specs=specs,
        out_specs=out_specs,
        out_shape=out_shape,
        scratch_shapes=[
            pltpu.VMEM((n, 2, size, size), jnp.float32),
            pltpu.VMEM((n * size, 2 * size), jnp.bfloat16),
            pltpu.VMEM((n * size, 2 * size), jnp.bfloat16),
            pltpu.VMEM((2 * size, n * size), jnp.bfloat16),
            pltpu.VMEM((2 * size, n * size), jnp.bfloat16),
            *rest.pop("scratch", []),
        ],
        compiler_params=pltpu.CompilerParams(vmem_limit_bytes=VMEM_LIMIT),
        cost_estimate=pl.CostEstimate(
            flops=flops, bytes_accessed=layers * 2 * 2 * 384 * size * 4, transcendentals=0
        ),
        name=name,
        **rest,
    )(*operands)


def entry(
    layers, groups, anchors, tables, wave, pieces, exts, starts, ends, tile_rows, name, after=None
):
    size = wave.shape[-1]
    count, n = len(layers), sum(map(len, groups))
    base = groups[0][0] if wave.shape[0] != n else 0
    operands = [anchors, wave, *tables]
    specs = [vmem()] * 4
    out_shape = [
        jax.ShapeDtypeStruct((len(group), 2, size, size), jnp.float32) for group in groups
    ]
    if pieces is not None:
        operands += [piece for piece, _ in pieces]
        for _, at in pieces:
            specs.append(
                pl.BlockSpec((count, 2, 2, size, size), lambda i, at=at: (at, 0, 0, 0, 0))
            )
        out_shape += [
            jax.ShapeDtypeStruct((2, 2, tile_rows + size, size), jnp.float32)
        ] * count
    else:
        operands += exts
        specs += [vmem()] * count
    kernel = functools.partial(
        entry_kernel, layers, groups, base, pieces is not None, starts, ends, after is not None
    )
    return call(
        kernel, operands, specs, out_shape, [vmem()] * len(out_shape), n, size, count, name,
        after=after,
    )


def first_section(tick, n, anchors, tables, probe_wave, exts, after, chunks):
    size = probe_wave.shape[-1]
    layers = list(range(len(exts)))
    return call(
        functools.partial(first_kernel, tick, layers),
        [anchors, probe_wave, *tables, *exts, after],
        [vmem()] * (4 + len(exts)) + [pl.BlockSpec(memory_space=pl.ANY)],
        jax.ShapeDtypeStruct((chunks * n, 2, size, size), jnp.float32),
        pl.BlockSpec((n, 2, size, size), lambda i: (i, 0, 0, 0)),
        n, size, len(exts), f"first{tick}", grid=(chunks,),
    )


def tick_section(
    tick, probes, anchors, tables, wave, exts, first, after, stored=(), out_shape=None, out=None
):
    size = wave.shape[-1]
    count, n = len(exts), len(probes)
    operands = [anchors, wave, *tables, *exts, first, *(part for _, part in stored)]
    specs = [vmem()] * (5 + count + len(stored))
    shape = [jax.ShapeDtypeStruct((n, 2, size, size), jnp.float32)]
    out_specs = [vmem()]
    rest = {"after": after}
    if out is not None:
        rest["input_output_aliases"] = {len(operands): 0}
        operands.append(out)
        specs.append(hbm())
        shape, out_specs = [jax.ShapeDtypeStruct(out.shape, out.dtype)], [hbm()]
        rest["scratch"] = [
            pltpu.VMEM((n, 2, size, size), jnp.float32),
            pltpu.SemaphoreType.DMA((len(stored) + 1,)),
        ]
    elif stored:
        shape.append(out_shape)
        out_specs.append(hbm())
        rest["scratch"] = [pltpu.SemaphoreType.DMA((len(stored),))]
    kernel = functools.partial(
        tick_kernel, tick, list(range(count)), probes, [to for to, _ in stored],
        out is not None, after is not None,
    )
    return call(
        kernel, operands, specs, shape, out_specs, n, size, count, f"tick{tick}_{probes[0]}", **rest
    )


def shards(phase_map, absorb, probe_wave, waves_in, scan_rows, scan_cols):
    size = probe_wave.shape[-1]
    slices, tile_rows = phase_map.shape[:2]
    tiles = lax.axis_size("tile")
    depth_count = lax.axis_size("depth")
    back = [(i, (i - 1) % tiles) for i in range(tiles)]
    onward = [(i, (i + 1) % depth_count) for i in range(depth_count)]

    firsts = edge_rows(phase_map, absorb, size)
    rims = [lax.ppermute(first, "tile", back) for first in firsts]
    rest = rest_rows(phase_map, absorb, size)

    tables = [jnp.asarray(table) for table in hop_tables(size)]
    depth, tile = lax.axis_index("depth"), lax.axis_index("tile")
    anchors = jnp.stack([scan_rows - tile * tile_rows, scan_cols], 1)
    anchors = lax.dynamic_slice_in_dim(anchors, depth_count - 1 - depth, TICKS, 0)
    anchors = jnp.broadcast_to(anchors.reshape(-1, 1), (anchors.size, size))
    held = waves_in[0]
    count = held.shape[0]
    exts = []
    done = []
    for r in range(slices):
        layers = [r]
        pieces = [(firsts[r], 0), (rest, r), (rims[r], 0)]
        edges = (r == 0, r == slices - 1, tile_rows)
        if r < slices - 1:
            held, *made = entry(
                layers, [list(range(count))], anchors, tables, held, pieces, None, *edges, f"enter{r}"
            )
            exts += made
            continue
        left, *made = entry(
            layers, GROUPS[:1], anchors, tables, held, pieces, None, *edges, "leave0"
        )
        exts += made
        done = [left]
        done += entry(
            layers, GROUPS[1:], anchors, tables, held, None, exts[-1:], *edges, "leave1", left
        )

    stored = []
    for tick in range(1, TICKS):
        stored += [((tick - 1, group[0]), part) for group, part in zip(GROUPS, done)]
        arrived = [lax.ppermute(left, "depth", onward) for left in done]
        first = first_section(tick, 1, anchors, tables, probe_wave, exts, done[-1], count)
        done = []
        for c, group in enumerate(GROUPS):
            last = {}
            if tick == TICKS - 1 and c == 0:
                shape = jax.ShapeDtypeStruct((TICKS, count, *held.shape[1:]), held.dtype)
                last = dict(stored=stored, out_shape=shape)
            elif tick == TICKS - 1 and c == len(GROUPS) - 1:
                stored = [((tick, other[0]), part) for other, part in zip(GROUPS, done)]
                last = dict(stored=stored, out=out)
            left, *made = tick_section(
                tick, group, anchors, tables, arrived[c], exts, first,
                done[-1] if done else None, **last
            )
            if made:
                out = made[0]
            done.append(left)
    out = done[-1]
    return out[:, None]


def solution(mesh):
    return jax.shard_map(
        shards,
        mesh=mesh,
        in_specs=(
            P("depth", "tile", None),
            P("depth", "tile", None),
            P(),
            P("depth", "tile", None, None, None),
            P(None, "tile"),
            P(None, "tile"),
        ),
        out_specs=P(None, "depth", "tile", None, None, None),
        check_vma=False,
    )
```

```python
import functools
import math

import jax
import jax.numpy as jnp
import ml_dtypes
import numpy as np
from jax import lax
from jax.experimental import pallas as pl
from jax.experimental.pallas import tpu as pltpu
from jax.sharding import PartitionSpec as P

TICKS = 3
GROUPS = [[0, 1], [2], [3]]

fresnel = 0.1
VMEM_LIMIT = 24 * 1024 * 1024
WEIGHT = 8
EDGE_LIMIT = VMEM_LIMIT

SIN_TERMS = [(-1.0) ** j / math.factorial(2 * j + 1) for j in range(7)]
COS_TERMS = [(-1.0) ** j / math.factorial(2 * j) for j in range(8)]


def hop_tables(size):
    index = np.arange(size)
    frequency = np.where(index < size // 2, index, index - size).astype(np.float64)
    k = np.exp(-1j * fresnel * math.pi * frequency**2 / size)
    lag = np.fft.ifft(k)
    g = lag[(index[:, None] - index[None, :]) % size]
    right = np.block([[g.real, g.imag], [-g.imag, g.real]])
    high = right.astype(ml_dtypes.bfloat16)
    low = (right - high.astype(np.float64)).astype(ml_dtypes.bfloat16)
    right = np.stack([high, low])
    return right, np.ascontiguousarray(right.transpose(0, 2, 1))


def series(z, terms):
    total = jnp.full_like(z, terms[-1])
    for term in terms[-2::-1]:
        total = total * z + term
    return total


def transmission(phase, absorb):
    t = 0.5 * phase
    z = t * t
    s = t * series(z, SIN_TERMS)
    c = series(z, COS_TERMS)
    damping = jnp.exp(-absorb)
    return damping * (1.0 - 2.0 * (s * s)), damping * (2.0 * (s * c))


def split(x):
    high = x.astype(jnp.bfloat16)
    return high, (x - high.astype(jnp.float32)).astype(jnp.bfloat16)


def product(a, b):
    return jnp.dot(a, b, preferred_element_type=jnp.float32)


def trans_layer(phase_ref, absorb_ref, out_ref):
    rows, columns = phase_ref.shape
    size = out_ref.shape[-1]
    step = 32

    def body(i, carry):
        at = pl.ds(pl.multiple_of(i * step, step), step)
        for half in range(columns // size):
            cols = slice(half * size, (half + 1) * size)
            real, imag = transmission(phase_ref[at, cols], absorb_ref[at, cols])
            out_ref[0, half, at, :] = real
            out_ref[1, half, at, :] = imag
        return carry

    lax.fori_loop(0, rows // step, body, 0)


def edge_kernel(first, phase_ref, absorb_ref, *refs):
    *out_refs, phase_buf, absorb_buf, sem = refs
    count, rows = phase_buf.shape[:2]
    copies = []
    for layer in range(count):
        for n, (ref, buf) in enumerate([(phase_ref, phase_buf), (absorb_ref, absorb_buf)]):
            source = ref.at[first + layer, pl.ds(0, rows)]
            copies.append(pltpu.make_async_copy(source, buf.at[layer], sem.at[2 * layer + n]))
            copies[-1].start()
    for layer in range(count):
        copies[2 * layer].wait()
        copies[2 * layer + 1].wait()
        trans_layer(phase_buf.at[layer], absorb_buf.at[layer], out_refs[layer].at[0])


def rest_kernel(phase_ref, absorb_ref, out_ref):
    for layer in range(phase_ref.shape[0]):
        trans_layer(phase_ref.at[layer], absorb_ref.at[layer], out_ref.at[layer])


def edge_rows(phase_map, absorb, size, layers):
    count, columns = len(layers), phase_map.shape[2]
    shape = jax.ShapeDtypeStruct((1, 2, columns // size, size, size), jnp.float32)
    values = count * size * columns
    return pl.pallas_call(
        functools.partial(edge_kernel, layers[0]),
        out_shape=[shape] * count,
        in_specs=[hbm()] * 2,
        out_specs=[vmem()] * count,
        scratch_shapes=[
            pltpu.VMEM((count, size, columns), jnp.float32),
            pltpu.VMEM((count, size, columns), jnp.float32),
            pltpu.SemaphoreType.DMA((2 * count,)),
        ],
        compiler_params=pltpu.CompilerParams(vmem_limit_bytes=EDGE_LIMIT),
        cost_estimate=pl.CostEstimate(
            flops=values * 40, bytes_accessed=values * 16, transcendentals=values
        ),
        name=f"edge{layers[0]}",
    )(*(pltpu.with_memory_space_constraint(x, pltpu.HBM) for x in (phase_map, absorb)))


def rest_rows(phase_map, absorb, size):
    count, rows, columns = phase_map.shape
    spec = pl.BlockSpec((count, rows - size, columns), lambda i: (0, 1, 0))
    values = count * (rows - size) * columns
    return pl.pallas_call(
        rest_kernel,
        grid=(1,),
        out_shape=jax.ShapeDtypeStruct((count, 2, columns // size, rows - size, size), jnp.float32),
        in_specs=[spec] * 2,
        out_specs=vmem(),
        compiler_params=pltpu.CompilerParams(vmem_limit_bytes=VMEM_LIMIT),
        cost_estimate=pl.CostEstimate(
            flops=values * 40, bytes_accessed=values * 16, transcendentals=values
        ),
        name="rest",
    )(phase_map, absorb)


def advance(
    tick, layers, probes, starts, ends, piece_refs, ext_refs, anchors_ref, waves, put, tables, scratch
):
    right_ref, left_ref = tables
    state, x_high, x_low, r_high, r_low = scratch
    size = state.shape[-1]
    each = anchors_ref.shape[0] // (2 * TICKS)
    row_at, col_at = [
        [anchors_ref[pl.ds((2 * tick + axis) * each + p, 1), :][0, 0] for p in probes]
        for axis in range(2)
    ]
    lane = lax.broadcasted_iota(jnp.int32, (size, size), 1)
    count = len(layers)

    for n in range(len(probes)):
        for part in range(2):
            wave = waves(n, part)
            if starts:
                wave = pltpu.roll(wave, col_at[n] & (size - 1), 1)
            state[n, part] = wave

    for j in range(count):
        ext = ext_refs[j]
        for piece, piece_ref in enumerate(piece_refs):
            rows = slice(piece * size, (piece + 1) * size)
            for part in range(2):
                for half in range(2):
                    ext[part, half, rows, :] = piece_ref[j, part, half]
        for n in range(len(probes)):
            at = pl.ds(row_at[n], size)
            inside = lane >= col_at[n]
            t_real = jnp.where(inside, ext[0, 0, at, :], ext[0, 1, at, :])
            t_imag = jnp.where(inside, ext[1, 0, at, :], ext[1, 1, at, :])
            real, imag = state[n, 0], state[n, 1]
            rows = slice(n * size, (n + 1) * size)
            x_high[rows, :size], x_low[rows, :size] = split(real * t_real - imag * t_imag)
            x_high[rows, size:], x_low[rows, size:] = split(real * t_imag + imag * t_real)
        y = (
            product(x_high[...], right_ref[0])
            + product(x_high[...], right_ref[1])
            + product(x_low[...], right_ref[0])
        )
        for n in range(len(probes)):
            rows = slice(n * size, (n + 1) * size)
            r_high[:size, rows], r_low[:size, rows] = split(y[rows, :size])
            r_high[size:, rows], r_low[size:, rows] = split(y[rows, size:])
        z = (
            product(left_ref[0], r_high[...])
            + product(left_ref[1], r_high[...])
            + product(left_ref[0], r_low[...])
        )
        for n in range(len(probes)):
            rows = slice(n * size, (n + 1) * size)
            for part in range(2):
                wave = z[part * size : (part + 1) * size, rows]
                if j < count - 1:
                    state[n, part] = wave
                    continue
                if ends:
                    wave = pltpu.roll(wave, (size - col_at[n]) & (size - 1), 1)
                put(n, part, wave)


def take(refs, count):
    return [refs.pop(0) for _ in range(count)]


def entry_kernel(layers, groups, base, with_pieces, starts, ends, with_after, *refs):
    refs = list(refs)
    anchors_ref, wave_ref, right_ref, left_ref = take(refs, 4)
    if with_pieces:
        piece_refs = take(refs, 3)
        take(refs, with_after)
        out_refs = take(refs, len(groups))
        ext_refs = take(refs, len(layers))
    else:
        piece_refs = []
        ext_refs = take(refs, len(layers))
        take(refs, with_after)
        out_refs = take(refs, len(groups))
    places = [(g, at) for g, group in enumerate(groups) for at in range(len(group))]

    def put(n, part, wave):
        g, at = places[n]
        out_refs[g][at, part] = wave

    advance(
        0, layers, sum(groups, []), starts, ends, piece_refs, ext_refs, anchors_ref,
        lambda n, part: wave_ref[base + n, part], put, (right_ref, left_ref), refs,
    )


def first_kernel(tick, layers, *refs):
    refs = list(refs)
    anchors_ref, probe_ref, right_ref, left_ref = take(refs, 4)
    ext_refs = take(refs, len(layers))
    _, out_ref = take(refs, 2)
    count = out_ref.shape[0]
    probes = [pl.program_id(0) * count + n for n in range(count)]

    def put(n, part, wave):
        out_ref[n, part] = wave

    @pl.when(lax.axis_index("depth") == 0)
    def _():
        advance(
            tick, layers, probes, True, True, [], ext_refs, anchors_ref,
            lambda n, part: probe_ref[part], put, (right_ref, left_ref), refs,
        )


def tick_kernel(tick, layers, probes, stores, own_store, with_after, *refs):
    refs = list(refs)
    anchors_ref, wave_ref, right_ref, left_ref = take(refs, 4)
    ext_refs = take(refs, len(layers))
    (first_ref,) = take(refs, 1)
    stored_refs = take(refs, len(stores))
    if own_store:
        take(refs, 1 + with_after)
        (final_ref,) = take(refs, 1)
        sem, out_ref = refs.pop(), refs.pop()
    elif stores:
        take(refs, with_after)
        out_ref, final_ref = take(refs, 2)
        sem = refs.pop()
    else:
        take(refs, with_after)
        (out_ref,) = take(refs, 1)

    copies = []
    for n, ((to, at), ref) in enumerate(zip(stores, stored_refs)):
        into = final_ref.at[to, pl.ds(at, ref.shape[0])]
        copies.append(pltpu.make_async_copy(ref, into, sem.at[n]))
        copies[-1].start()

    def put(n, part, wave):
        out_ref[n, part] = wave

    depth = lax.axis_index("depth")

    @pl.when(depth == 0)
    def _():
        out_ref[...] = first_ref[probes[0] : probes[0] + len(probes)]

    @pl.when(depth != 0)
    def _():
        advance(
            tick, layers, probes, True, True, [], ext_refs, anchors_ref,
            lambda n, part: wave_ref[n, part], put, (right_ref, left_ref), refs,
        )

    if own_store:
        into = final_ref.at[tick, pl.ds(probes[0], len(probes))]
        copies.append(pltpu.make_async_copy(out_ref, into, sem.at[len(stores)]))
        copies[-1].start()
    for copy in copies:
        copy.wait()


def vmem():
    return pl.BlockSpec(memory_space=pltpu.VMEM)


def hbm():
    return pl.BlockSpec(memory_space=pltpu.HBM)


def call(kernel, operands, specs, out_shape, out_specs, n, size, layers, name, **rest):
    grid = rest.pop("grid", (1,))
    flops = WEIGHT * grid[0] * layers * n * 2 * 3 * 2 * size * (2 * size) ** 2
    after = rest.pop("after", None)
    if after is not None:
        operands.append(after)
        specs.append(pl.BlockSpec(memory_space=pl.ANY))
    return pl.pallas_call(
        kernel,
        grid=grid,
        in_specs=specs,
        out_specs=out_specs,
        out_shape=out_shape,
        scratch_shapes=[
            pltpu.VMEM((n, 2, size, size), jnp.float32),
            pltpu.VMEM((n * size, 2 * size), jnp.bfloat16),
            pltpu.VMEM((n * size, 2 * size), jnp.bfloat16),
            pltpu.VMEM((2 * size, n * size), jnp.bfloat16),
            pltpu.VMEM((2 * size, n * size), jnp.bfloat16),
            *rest.pop("scratch", []),
        ],
        compiler_params=pltpu.CompilerParams(vmem_limit_bytes=VMEM_LIMIT),
        cost_estimate=pl.CostEstimate(
            flops=flops, bytes_accessed=layers * 2 * 2 * 384 * size * 4, transcendentals=0
        ),
        name=name,
        **rest,
    )(*operands)


def entry(
    layers, groups, anchors, tables, wave, pieces, exts, starts, ends, tile_rows, name, after=None
):
    size = wave.shape[-1]
    count, n = len(layers), sum(map(len, groups))
    base = groups[0][0] if wave.shape[0] != n else 0
    operands = [anchors, wave, *tables]
    specs = [vmem()] * 4
    out_shape = [
        jax.ShapeDtypeStruct((len(group), 2, size, size), jnp.float32) for group in groups
    ]
    if pieces is not None:
        operands += [piece for piece, _ in pieces]
        for _, at in pieces:
            specs.append(
                pl.BlockSpec((count, 2, 2, size, size), lambda i, at=at: (at, 0, 0, 0, 0))
            )
        out_shape += [
            jax.ShapeDtypeStruct((2, 2, tile_rows + size, size), jnp.float32)
        ] * count
    else:
        operands += exts
        specs += [vmem()] * count
    kernel = functools.partial(
        entry_kernel, layers, groups, base, pieces is not None, starts, ends, after is not None
    )
    return call(
        kernel, operands, specs, out_shape, [vmem()] * len(out_shape), n, size, count, name,
        after=after,
    )


def first_section(tick, n, anchors, tables, probe_wave, exts, after, chunks):
    size = probe_wave.shape[-1]
    layers = list(range(len(exts)))
    return call(
        functools.partial(first_kernel, tick, layers),
        [anchors, probe_wave, *tables, *exts, after],
        [vmem()] * (4 + len(exts)) + [pl.BlockSpec(memory_space=pl.ANY)],
        jax.ShapeDtypeStruct((chunks * n, 2, size, size), jnp.float32),
        pl.BlockSpec((n, 2, size, size), lambda i: (i, 0, 0, 0)),
        n, size, len(exts), f"first{tick}", grid=(chunks,),
    )


def tick_section(
    tick, probes, anchors, tables, wave, exts, first, after, stored=(), out_shape=None, out=None
):
    size = wave.shape[-1]
    count, n = len(exts), len(probes)
    operands = [anchors, wave, *tables, *exts, first, *(part for _, part in stored)]
    specs = [vmem()] * (5 + count + len(stored))
    shape = [jax.ShapeDtypeStruct((n, 2, size, size), jnp.float32)]
    out_specs = [vmem()]
    rest = {"after": after}
    if out is not None:
        rest["input_output_aliases"] = {len(operands): 0}
        operands.append(out)
        specs.append(hbm())
        shape, out_specs = [jax.ShapeDtypeStruct(out.shape, out.dtype)], [hbm()]
        rest["scratch"] = [
            pltpu.VMEM((n, 2, size, size), jnp.float32),
            pltpu.SemaphoreType.DMA((len(stored) + 1,)),
        ]
    elif stored:
        shape.append(out_shape)
        out_specs.append(hbm())
        rest["scratch"] = [pltpu.SemaphoreType.DMA((len(stored),))]
    kernel = functools.partial(
        tick_kernel, tick, list(range(count)), probes, [to for to, _ in stored],
        out is not None, after is not None,
    )
    return call(
        kernel, operands, specs, shape, out_specs, n, size, count, f"tick{tick}_{probes[0]}", **rest
    )


def shards(phase_map, absorb, probe_wave, waves_in, scan_rows, scan_cols):
    size = probe_wave.shape[-1]
    slices, tile_rows = phase_map.shape[:2]
    tiles = lax.axis_size("tile")
    depth_count = lax.axis_size("depth")
    back = [(i, (i - 1) % tiles) for i in range(tiles)]
    onward = [(i, (i + 1) % depth_count) for i in range(depth_count)]

    firsts = edge_rows(phase_map, absorb, size, [0])
    firsts += edge_rows(phase_map, absorb, size, list(range(1, slices)))
    rims = [lax.ppermute(first, "tile", back) for first in firsts]
    rest = rest_rows(phase_map, absorb, size)

    tables = [jnp.asarray(table) for table in hop_tables(size)]
    depth, tile = lax.axis_index("depth"), lax.axis_index("tile")
    anchors = jnp.stack([scan_rows - tile * tile_rows, scan_cols], 1)
    anchors = lax.dynamic_slice_in_dim(anchors, depth_count - 1 - depth, TICKS, 0)
    anchors = jnp.broadcast_to(anchors.reshape(-1, 1), (anchors.size, size))
    held = waves_in[0]
    count = held.shape[0]
    exts = []
    done = []
    for r in range(slices):
        layers = [r]
        pieces = [(firsts[r], 0), (rest, r), (rims[r], 0)]
        edges = (r == 0, r == slices - 1, tile_rows)
        if r < slices - 1:
            held, *made = entry(
                layers, [list(range(count))], anchors, tables, held, pieces, None, *edges, f"enter{r}"
            )
            exts += made
            continue
        left, *made = entry(
            layers, GROUPS[:1], anchors, tables, held, pieces, None, *edges, "leave0"
        )
        exts += made
        done = [left]
        done += entry(
            layers, GROUPS[1:], anchors, tables, held, None, exts[-1:], *edges, "leave1", left
        )

    stored = []
    for tick in range(1, TICKS):
        stored += [((tick - 1, group[0]), part) for group, part in zip(GROUPS, done)]
        arrived = [lax.ppermute(left, "depth", onward) for left in done]
        first = first_section(
            tick, 2, anchors, tables, probe_wave, exts, done[-1], count // 2
        )
        done = []
        for c, group in enumerate(GROUPS):
            last = {}
            if tick == TICKS - 1 and c == 0:
                shape = jax.ShapeDtypeStruct((TICKS, count, *held.shape[1:]), held.dtype)
                last = dict(stored=stored, out_shape=shape)
            elif tick == TICKS - 1 and c == len(GROUPS) - 1:
                stored = [((tick, other[0]), part) for other, part in zip(GROUPS, done)]
                last = dict(stored=stored, out=out)
            left, *made = tick_section(
                tick, group, anchors, tables, arrived[c], exts, first,
                done[-1] if done else None, **last
            )
            if made:
                out = made[0]
            done.append(left)
    out = done[-1]
    return out[:, None]


def solution(mesh):
    return jax.shard_map(
        shards,
        mesh=mesh,
        in_specs=(
            P("depth", "tile", None),
            P("depth", "tile", None),
            P(),
            P("depth", "tile", None, None, None),
            P(None, "tile"),
            P(None, "tile"),
        ),
        out_specs=P(None, "depth", "tile", None, None, None),
        check_vma=False,
    )
```

```python
import functools
import math

import jax
import jax.numpy as jnp
import ml_dtypes
import numpy as np
from jax import lax
from jax.experimental import pallas as pl
from jax.experimental.pallas import tpu as pltpu
from jax.sharding import PartitionSpec as P

TICKS = 3
GROUPS = [[0, 1], [2], [3]]

fresnel = 0.1
VMEM_LIMIT = 24 * 1024 * 1024
WEIGHT = 8
EDGE_LIMIT = VMEM_LIMIT

SIN_TERMS = [(-1.0) ** j / math.factorial(2 * j + 1) for j in range(7)]
COS_TERMS = [(-1.0) ** j / math.factorial(2 * j) for j in range(8)]


def hop_tables(size):
    index = np.arange(size)
    frequency = np.where(index < size // 2, index, index - size).astype(np.float64)
    k = np.exp(-1j * fresnel * math.pi * frequency**2 / size)
    lag = np.fft.ifft(k)
    g = lag[(index[:, None] - index[None, :]) % size]
    right = np.block([[g.real, g.imag], [-g.imag, g.real]])
    high = right.astype(ml_dtypes.bfloat16)
    low = (right - high.astype(np.float64)).astype(ml_dtypes.bfloat16)
    right = np.stack([high, low])
    left = right.transpose(0, 2, 1)
    columns = left[:, :, :size]
    single = np.concatenate([columns[0], columns[0], columns[1]], 1)
    return right, left.reshape(4 * size, 2 * size), single


def series(z, terms):
    total = jnp.full_like(z, terms[-1])
    for term in terms[-2::-1]:
        total = total * z + term
    return total


def transmission(phase, absorb):
    t = 0.5 * phase
    z = t * t
    s = t * series(z, SIN_TERMS)
    c = series(z, COS_TERMS)
    damping = jnp.exp(-absorb)
    return damping * (1.0 - 2.0 * (s * s)), damping * (2.0 * (s * c))


def split(x):
    high = x.astype(jnp.bfloat16)
    return high, (x - high.astype(jnp.float32)).astype(jnp.bfloat16)


def product(a, b):
    return jnp.dot(a, b, preferred_element_type=jnp.float32)


def trans_layer(phase_ref, absorb_ref, out_ref):
    rows, columns = phase_ref.shape
    size = out_ref.shape[-1]
    step = 32

    def body(i, carry):
        at = pl.ds(pl.multiple_of(i * step, step), step)
        for half in range(columns // size):
            cols = slice(half * size, (half + 1) * size)
            real, imag = transmission(phase_ref[at, cols], absorb_ref[at, cols])
            out_ref[0, half, at, :] = real
            out_ref[1, half, at, :] = imag
        return carry

    lax.fori_loop(0, rows // step, body, 0)


def edge_kernel(first, phase_ref, absorb_ref, *refs):
    *out_refs, phase_buf, absorb_buf, sem = refs
    count, rows = phase_buf.shape[:2]
    copies = []
    for layer in range(count):
        for n, (ref, buf) in enumerate([(phase_ref, phase_buf), (absorb_ref, absorb_buf)]):
            source = ref.at[first + layer, pl.ds(0, rows)]
            copies.append(pltpu.make_async_copy(source, buf.at[layer], sem.at[2 * layer + n]))
            copies[-1].start()
    for layer in range(count):
        copies[2 * layer].wait()
        copies[2 * layer + 1].wait()
        trans_layer(phase_buf.at[layer], absorb_buf.at[layer], out_refs[layer].at[0])


def rest_kernel(phase_ref, absorb_ref, out_ref):
    for layer in range(phase_ref.shape[0]):
        trans_layer(phase_ref.at[layer], absorb_ref.at[layer], out_ref.at[layer])


def edge_rows(phase_map, absorb, size, layers):
    count, columns = len(layers), phase_map.shape[2]
    shape = jax.ShapeDtypeStruct((1, 2, columns // size, size, size), jnp.float32)
    values = count * size * columns
    return pl.pallas_call(
        functools.partial(edge_kernel, layers[0]),
        out_shape=[shape] * count,
        in_specs=[hbm()] * 2,
        out_specs=[vmem()] * count,
        scratch_shapes=[
            pltpu.VMEM((count, size, columns), jnp.float32),
            pltpu.VMEM((count, size, columns), jnp.float32),
            pltpu.SemaphoreType.DMA((2 * count,)),
        ],
        compiler_params=pltpu.CompilerParams(vmem_limit_bytes=EDGE_LIMIT),
        cost_estimate=pl.CostEstimate(
            flops=values * 40, bytes_accessed=values * 16, transcendentals=values
        ),
        name=f"edge{layers[0]}",
    )(*(pltpu.with_memory_space_constraint(x, pltpu.HBM) for x in (phase_map, absorb)))


def rest_rows(phase_map, absorb, size):
    count, rows, columns = phase_map.shape
    spec = pl.BlockSpec((count, rows - size, columns), lambda i: (0, 1, 0))
    values = count * (rows - size) * columns
    return pl.pallas_call(
        rest_kernel,
        grid=(1,),
        out_shape=jax.ShapeDtypeStruct((count, 2, columns // size, rows - size, size), jnp.float32),
        in_specs=[spec] * 2,
        out_specs=vmem(),
        compiler_params=pltpu.CompilerParams(vmem_limit_bytes=VMEM_LIMIT),
        cost_estimate=pl.CostEstimate(
            flops=values * 40, bytes_accessed=values * 16, transcendentals=values
        ),
        name="rest",
    )(phase_map, absorb)


def advance(
    tick, layers, probes, starts, ends, piece_refs, ext_refs, anchors_ref, waves, put, tables, scratch
):
    right_ref, left_ref = tables
    state, x_all, r_high, r_low = scratch
    size = state.shape[-1]
    each = anchors_ref.shape[0] // (2 * TICKS)
    row_at, col_at = [
        [anchors_ref[pl.ds((2 * tick + axis) * each + p, 1), :][0, 0] for p in probes]
        for axis in range(2)
    ]
    lane = lax.broadcasted_iota(jnp.int32, (size, size), 1)
    count, total = len(layers), len(probes) * size

    for n in range(len(probes)):
        for part in range(2):
            wave = waves(n, part)
            if starts:
                wave = pltpu.roll(wave, col_at[n] & (size - 1), 1)
            state[n, part] = wave

    def leave(n, part, j, wave):
        if j < count - 1:
            state[n, part] = wave
            return
        if ends:
            wave = pltpu.roll(wave, (size - col_at[n]) & (size - 1), 1)
        put(n, part, wave)

    for j in range(count):
        ext = ext_refs[j]
        for piece, piece_ref in enumerate(piece_refs):
            rows = slice(piece * size, (piece + 1) * size)
            for part in range(2):
                for half in range(2):
                    ext[part, half, rows, :] = piece_ref[j, part, half]
        for n in range(len(probes)):
            at = pl.ds(row_at[n], size)
            inside = lane >= col_at[n]
            t_real = jnp.where(inside, ext[0, 0, at, :], ext[0, 1, at, :])
            t_imag = jnp.where(inside, ext[1, 0, at, :], ext[1, 1, at, :])
            real, imag = state[n, 0], state[n, 1]
            rows = slice(n * size, (n + 1) * size)
            lows = slice(total + n * size, total + (n + 1) * size)
            x_all[rows, :size], x_all[lows, :size] = split(real * t_real - imag * t_imag)
            x_all[rows, size:], x_all[lows, size:] = split(real * t_imag + imag * t_real)
        both = product(x_all[...], right_ref[0])
        y = both[:total] + (both[total:] + product(x_all[:total], right_ref[1]))
        if len(probes) == 1:
            high, low = split(y)
            r_high[:size], r_high[size : 2 * size], r_high[2 * size :] = high, low, high
            s = product(left_ref[...], r_high[...])
            parts = (s[:size, :size] - s[size:, size:], s[size:, :size] + s[:size, size:])
            for part in range(2):
                leave(0, part, j, parts[part])
            continue
        for n in range(len(probes)):
            rows = slice(n * size, (n + 1) * size)
            r_high[:size, rows], r_low[:size, rows] = split(y[rows, :size])
            r_high[size:, rows], r_low[size:, rows] = split(y[rows, size:])
        both = product(left_ref[...], r_high[...])
        width = 2 * size
        z = both[:width] + (both[width:] + product(left_ref[:width], r_low[...]))
        for n in range(len(probes)):
            rows = slice(n * size, (n + 1) * size)
            for part in range(2):
                leave(n, part, j, z[part * size : (part + 1) * size, rows])


def take(refs, count):
    return [refs.pop(0) for _ in range(count)]


def entry_kernel(layers, groups, base, with_pieces, starts, ends, with_after, *refs):
    refs = list(refs)
    anchors_ref, wave_ref, right_ref, left_ref = take(refs, 4)
    if with_pieces:
        piece_refs = take(refs, 3)
        take(refs, with_after)
        out_refs = take(refs, len(groups))
        ext_refs = take(refs, len(layers))
    else:
        piece_refs = []
        ext_refs = take(refs, len(layers))
        take(refs, with_after)
        out_refs = take(refs, len(groups))
    places = [(g, at) for g, group in enumerate(groups) for at in range(len(group))]

    def put(n, part, wave):
        g, at = places[n]
        out_refs[g][at, part] = wave

    advance(
        0, layers, sum(groups, []), starts, ends, piece_refs, ext_refs, anchors_ref,
        lambda n, part: wave_ref[base + n, part], put, (right_ref, left_ref), refs,
    )


def first_kernel(tick, layers, *refs):
    refs = list(refs)
    anchors_ref, probe_ref, right_ref, left_ref = take(refs, 4)
    ext_refs = take(refs, len(layers))
    _, out_ref = take(refs, 2)
    count = out_ref.shape[0]
    probes = [pl.program_id(0) * count + n for n in range(count)]

    def put(n, part, wave):
        out_ref[n, part] = wave

    @pl.when(lax.axis_index("depth") == 0)
    def _():
        advance(
            tick, layers, probes, True, True, [], ext_refs, anchors_ref,
            lambda n, part: probe_ref[part], put, (right_ref, left_ref), refs,
        )


def tick_kernel(tick, layers, probes, stores, own_store, with_after, *refs):
    refs = list(refs)
    anchors_ref, wave_ref, right_ref, left_ref = take(refs, 4)
    ext_refs = take(refs, len(layers))
    (first_ref,) = take(refs, 1)
    stored_refs = take(refs, len(stores))
    if own_store:
        take(refs, 1 + with_after)
        (final_ref,) = take(refs, 1)
        sem, out_ref = refs.pop(), refs.pop()
    elif stores:
        take(refs, with_after)
        out_ref, final_ref = take(refs, 2)
        sem = refs.pop()
    else:
        take(refs, with_after)
        (out_ref,) = take(refs, 1)

    copies = []
    for n, ((to, at), ref) in enumerate(zip(stores, stored_refs)):
        into = final_ref.at[to, pl.ds(at, ref.shape[0])]
        copies.append(pltpu.make_async_copy(ref, into, sem.at[n]))
        copies[-1].start()

    def put(n, part, wave):
        out_ref[n, part] = wave

    depth = lax.axis_index("depth")

    @pl.when(depth == 0)
    def _():
        out_ref[...] = first_ref[probes[0] : probes[0] + len(probes)]

    @pl.when(depth != 0)
    def _():
        advance(
            tick, layers, probes, True, True, [], ext_refs, anchors_ref,
            lambda n, part: wave_ref[n, part], put, (right_ref, left_ref), refs,
        )

    if own_store:
        into = final_ref.at[tick, pl.ds(probes[0], len(probes))]
        copies.append(pltpu.make_async_copy(out_ref, into, sem.at[len(stores)]))
        copies[-1].start()
    for copy in copies:
        copy.wait()


def vmem():
    return pl.BlockSpec(memory_space=pltpu.VMEM)


def hbm():
    return pl.BlockSpec(memory_space=pltpu.HBM)


def pick(tables, n):
    right, left, single = tables
    return right, single if n == 1 else left


def call(kernel, operands, specs, out_shape, out_specs, n, size, layers, name, **rest):
    grid = rest.pop("grid", (1,))
    flops = WEIGHT * grid[0] * layers * n * 2 * 3 * 2 * size * (2 * size) ** 2
    after = rest.pop("after", None)
    if after is not None:
        operands.append(after)
        specs.append(pl.BlockSpec(memory_space=pl.ANY))
    return pl.pallas_call(
        kernel,
        grid=grid,
        in_specs=specs,
        out_specs=out_specs,
        out_shape=out_shape,
        scratch_shapes=[
            pltpu.VMEM((n, 2, size, size), jnp.float32),
            pltpu.VMEM((2 * n * size, 2 * size), jnp.bfloat16),
            pltpu.VMEM((3 * size, 2 * size) if n == 1 else (2 * size, n * size), jnp.bfloat16),
            pltpu.VMEM((2 * size, n * size), jnp.bfloat16),
            *rest.pop("scratch", []),
        ],
        compiler_params=pltpu.CompilerParams(vmem_limit_bytes=VMEM_LIMIT),
        cost_estimate=pl.CostEstimate(
            flops=flops, bytes_accessed=layers * 2 * 2 * 384 * size * 4, transcendentals=0
        ),
        name=name,
        **rest,
    )(*operands)


def entry(
    layers, groups, anchors, tables, wave, pieces, exts, starts, ends, tile_rows, name, after=None
):
    size = wave.shape[-1]
    count, n = len(layers), sum(map(len, groups))
    base = groups[0][0] if wave.shape[0] != n else 0
    operands = [anchors, wave, *pick(tables, n)]
    specs = [vmem()] * 4
    out_shape = [
        jax.ShapeDtypeStruct((len(group), 2, size, size), jnp.float32) for group in groups
    ]
    if pieces is not None:
        operands += [piece for piece, _ in pieces]
        for _, at in pieces:
            specs.append(
                pl.BlockSpec((count, 2, 2, size, size), lambda i, at=at: (at, 0, 0, 0, 0))
            )
        out_shape += [
            jax.ShapeDtypeStruct((2, 2, tile_rows + size, size), jnp.float32)
        ] * count
    else:
        operands += exts
        specs += [vmem()] * count
    kernel = functools.partial(
        entry_kernel, layers, groups, base, pieces is not None, starts, ends, after is not None
    )
    return call(
        kernel, operands, specs, out_shape, [vmem()] * len(out_shape), n, size, count, name,
        after=after,
    )


def first_section(tick, n, anchors, tables, probe_wave, exts, after, chunks):
    size = probe_wave.shape[-1]
    layers = list(range(len(exts)))
    return call(
        functools.partial(first_kernel, tick, layers),
        [anchors, probe_wave, *pick(tables, n), *exts, after],
        [vmem()] * (4 + len(exts)) + [pl.BlockSpec(memory_space=pl.ANY)],
        jax.ShapeDtypeStruct((chunks * n, 2, size, size), jnp.float32),
        pl.BlockSpec((n, 2, size, size), lambda i: (i, 0, 0, 0)),
        n, size, len(exts), f"first{tick}", grid=(chunks,),
    )


def tick_section(
    tick, probes, anchors, tables, wave, exts, first, after, stored=(), out_shape=None, out=None
):
    size = wave.shape[-1]
    count, n = len(exts), len(probes)
    operands = [anchors, wave, *pick(tables, n), *exts, first, *(part for _, part in stored)]
    specs = [vmem()] * (5 + count + len(stored))
    shape = [jax.ShapeDtypeStruct((n, 2, size, size), jnp.float32)]
    out_specs = [vmem()]
    rest = {"after": after}
    if out is not None:
        rest["input_output_aliases"] = {len(operands): 0}
        operands.append(out)
        specs.append(hbm())
        shape, out_specs = [jax.ShapeDtypeStruct(out.shape, out.dtype)], [hbm()]
        rest["scratch"] = [
            pltpu.VMEM((n, 2, size, size), jnp.float32),
            pltpu.SemaphoreType.DMA((len(stored) + 1,)),
        ]
    elif stored:
        shape.append(out_shape)
        out_specs.append(hbm())
        rest["scratch"] = [pltpu.SemaphoreType.DMA((len(stored),))]
    kernel = functools.partial(
        tick_kernel, tick, list(range(count)), probes, [to for to, _ in stored],
        out is not None, after is not None,
    )
    return call(
        kernel, operands, specs, shape, out_specs, n, size, count, f"tick{tick}_{probes[0]}", **rest
    )


def shards(phase_map, absorb, probe_wave, waves_in, scan_rows, scan_cols):
    size = probe_wave.shape[-1]
    slices, tile_rows = phase_map.shape[:2]
    tiles = lax.axis_size("tile")
    depth_count = lax.axis_size("depth")
    back = [(i, (i - 1) % tiles) for i in range(tiles)]
    onward = [(i, (i + 1) % depth_count) for i in range(depth_count)]

    firsts = edge_rows(phase_map, absorb, size, [0])
    firsts += edge_rows(phase_map, absorb, size, list(range(1, slices)))
    rims = [lax.ppermute(first, "tile", back) for first in firsts]
    rest = rest_rows(phase_map, absorb, size)

    tables = [jnp.asarray(table) for table in hop_tables(size)]
    depth, tile = lax.axis_index("depth"), lax.axis_index("tile")
    anchors = jnp.stack([scan_rows - tile * tile_rows, scan_cols], 1)
    anchors = lax.dynamic_slice_in_dim(anchors, depth_count - 1 - depth, TICKS, 0)
    anchors = jnp.broadcast_to(anchors.reshape(-1, 1), (anchors.size, size))
    held = waves_in[0]
    count = held.shape[0]
    exts = []
    done = []
    for r in range(slices):
        layers = [r]
        pieces = [(firsts[r], 0), (rest, r), (rims[r], 0)]
        edges = (r == 0, r == slices - 1, tile_rows)
        if r < slices - 1:
            held, *made = entry(
                layers, [list(range(count))], anchors, tables, held, pieces, None, *edges, f"enter{r}"
            )
            exts += made
            continue
        left, *made = entry(
            layers, GROUPS[:1], anchors, tables, held, pieces, None, *edges, "leave0"
        )
        exts += made
        done = [left]
        done += entry(
            layers, GROUPS[1:], anchors, tables, held, None, exts[-1:], *edges, "leave1", left
        )

    stored = []
    for tick in range(1, TICKS):
        stored += [((tick - 1, group[0]), part) for group, part in zip(GROUPS, done)]
        arrived = [lax.ppermute(left, "depth", onward) for left in done]
        first = first_section(
            tick, 2, anchors, tables, probe_wave, exts, done[-1], count // 2
        )
        done = []
        for c, group in enumerate(GROUPS):
            last = {}
            if tick == TICKS - 1 and c == 0:
                shape = jax.ShapeDtypeStruct((TICKS, count, *held.shape[1:]), held.dtype)
                last = dict(stored=stored, out_shape=shape)
            elif tick == TICKS - 1 and c == len(GROUPS) - 1:
                stored = [((tick, other[0]), part) for other, part in zip(GROUPS, done)]
                last = dict(stored=stored, out=out)
            left, *made = tick_section(
                tick, group, anchors, tables, arrived[c], exts, first,
                done[-1] if done else None, **last
            )
            if made:
                out = made[0]
            done.append(left)
    out = done[-1]
    return out[:, None]


def solution(mesh):
    return jax.shard_map(
        shards,
        mesh=mesh,
        in_specs=(
            P("depth", "tile", None),
            P("depth", "tile", None),
            P(),
            P("depth", "tile", None, None, None),
            P(None, "tile"),
            P(None, "tile"),
        ),
        out_specs=P(None, "depth", "tile", None, None, None),
        check_vma=False,
    )
```

```python
import functools
import math

import jax
import jax.numpy as jnp
import ml_dtypes
import numpy as np
from jax import lax
from jax.experimental import pallas as pl
from jax.experimental.pallas import tpu as pltpu
from jax.sharding import PartitionSpec as P

TICKS = 3
GROUPS = [[0, 1], [2], [3]]

fresnel = 0.1
VMEM_LIMIT = 24 * 1024 * 1024
WEIGHT = 8
EDGE_LIMIT = VMEM_LIMIT

SIN_TERMS = [(-1.0) ** j / math.factorial(2 * j + 1) for j in range(7)]
COS_TERMS = [(-1.0) ** j / math.factorial(2 * j) for j in range(8)]


def hop_tables(size):
    index = np.arange(size)
    frequency = np.where(index < size // 2, index, index - size).astype(np.float64)
    k = np.exp(-1j * fresnel * math.pi * frequency**2 / size)
    lag = np.fft.ifft(k)
    g = lag[(index[:, None] - index[None, :]) % size]
    right = np.block([[g.real, g.imag], [-g.imag, g.real]])
    high = right.astype(ml_dtypes.bfloat16)
    low = (right - high.astype(np.float64)).astype(ml_dtypes.bfloat16)
    right = np.stack([high, low])
    left = right.transpose(0, 2, 1)
    columns = left[:, :, :size]
    single = np.concatenate([columns[0], columns[0], columns[1]], 1)
    return right, left.reshape(4 * size, 2 * size), single


def series(z, terms):
    total = jnp.full_like(z, terms[-1])
    for term in terms[-2::-1]:
        total = total * z + term
    return total


def transmission(phase, absorb):
    t = 0.5 * phase
    z = t * t
    s = t * series(z, SIN_TERMS)
    c = series(z, COS_TERMS)
    damping = jnp.exp(-absorb)
    return damping * (1.0 - 2.0 * (s * s)), damping * (2.0 * (s * c))


def split(x):
    high = x.astype(jnp.bfloat16)
    return high, (x - high.astype(jnp.float32)).astype(jnp.bfloat16)


def product(a, b):
    return jnp.dot(a, b, preferred_element_type=jnp.float32)


def trans_layer(phase_ref, absorb_ref, out_ref):
    rows, columns = phase_ref.shape
    size = out_ref.shape[-1]
    step = 32

    def body(i, carry):
        at = pl.ds(pl.multiple_of(i * step, step), step)
        for half in range(columns // size):
            cols = slice(half * size, (half + 1) * size)
            real, imag = transmission(phase_ref[at, cols], absorb_ref[at, cols])
            out_ref[0, half, at, :] = real
            out_ref[1, half, at, :] = imag
        return carry

    lax.fori_loop(0, rows // step, body, 0)


def edge_kernel(first, phase_ref, absorb_ref, *refs):
    *out_refs, phase_buf, absorb_buf, sem = refs
    count, rows = phase_buf.shape[:2]
    copies = []
    for layer in range(count):
        for n, (ref, buf) in enumerate([(phase_ref, phase_buf), (absorb_ref, absorb_buf)]):
            source = ref.at[first + layer, pl.ds(0, rows)]
            copies.append(pltpu.make_async_copy(source, buf.at[layer], sem.at[2 * layer + n]))
            copies[-1].start()
    for layer in range(count):
        copies[2 * layer].wait()
        copies[2 * layer + 1].wait()
        trans_layer(phase_buf.at[layer], absorb_buf.at[layer], out_refs[layer].at[0])


def rest_kernel(phase_ref, absorb_ref, out_ref):
    for layer in range(phase_ref.shape[0]):
        trans_layer(phase_ref.at[layer], absorb_ref.at[layer], out_ref.at[layer])


def edge_rows(phase_map, absorb, size, layers):
    count, columns = len(layers), phase_map.shape[2]
    shape = jax.ShapeDtypeStruct((1, 2, columns // size, size, size), jnp.float32)
    values = count * size * columns
    return pl.pallas_call(
        functools.partial(edge_kernel, layers[0]),
        out_shape=[shape] * count,
        in_specs=[hbm()] * 2,
        out_specs=[vmem()] * count,
        scratch_shapes=[
            pltpu.VMEM((count, size, columns), jnp.float32),
            pltpu.VMEM((count, size, columns), jnp.float32),
            pltpu.SemaphoreType.DMA((2 * count,)),
        ],
        compiler_params=pltpu.CompilerParams(vmem_limit_bytes=EDGE_LIMIT),
        cost_estimate=pl.CostEstimate(
            flops=values * 40, bytes_accessed=values * 16, transcendentals=values
        ),
        name=f"edge{layers[0]}",
    )(*(pltpu.with_memory_space_constraint(x, pltpu.HBM) for x in (phase_map, absorb)))


def rest_rows(phase_map, absorb, size):
    count, rows, columns = phase_map.shape
    spec = pl.BlockSpec((count, rows - size, columns), lambda i: (0, 1, 0))
    values = count * (rows - size) * columns
    return pl.pallas_call(
        rest_kernel,
        grid=(1,),
        out_shape=jax.ShapeDtypeStruct((count, 2, columns // size, rows - size, size), jnp.float32),
        in_specs=[spec] * 2,
        out_specs=vmem(),
        compiler_params=pltpu.CompilerParams(vmem_limit_bytes=VMEM_LIMIT),
        cost_estimate=pl.CostEstimate(
            flops=values * 40, bytes_accessed=values * 16, transcendentals=values
        ),
        name="rest",
    )(phase_map, absorb)


def advance(
    tick, layers, probes, starts, ends, piece_refs, ext_refs, anchors_ref, waves, put, tables, scratch
):
    right_ref, left_ref = tables
    state, x_all, r_high, r_low = scratch
    size = state.shape[-1]
    each = anchors_ref.shape[0] // (2 * TICKS)
    row_at, col_at = [
        [anchors_ref[pl.ds((2 * tick + axis) * each + p, 1), :][0, 0] for p in probes]
        for axis in range(2)
    ]
    lane = lax.broadcasted_iota(jnp.int32, (size, size), 1)
    count, total = len(layers), len(probes) * size

    for n in range(len(probes)):
        for part in range(2):
            wave = waves(n, part)
            if starts:
                wave = pltpu.roll(wave, col_at[n] & (size - 1), 1)
            state[n, part] = wave

    def leave(n, part, j, wave):
        if j < count - 1:
            state[n, part] = wave
            return
        if ends:
            wave = pltpu.roll(wave, (size - col_at[n]) & (size - 1), 1)
        put(n, part, wave)

    for j in range(count):
        ext = ext_refs[j]
        for piece, piece_ref in enumerate(piece_refs):
            rows = slice(piece * size, (piece + 1) * size)
            for part in range(2):
                for half in range(2):
                    ext[part, half, rows, :] = piece_ref[j, part, half]
        for n in range(len(probes)):
            at = pl.ds(row_at[n], size)
            inside = lane >= col_at[n]
            t_real = jnp.where(inside, ext[0, 0, at, :], ext[0, 1, at, :])
            t_imag = jnp.where(inside, ext[1, 0, at, :], ext[1, 1, at, :])
            real, imag = state[n, 0], state[n, 1]
            rows = slice(n * size, (n + 1) * size)
            lows = slice(total + n * size, total + (n + 1) * size)
            x_all[rows, :size], x_all[lows, :size] = split(real * t_real - imag * t_imag)
            x_all[rows, size:], x_all[lows, size:] = split(real * t_imag + imag * t_real)
        both = product(x_all[...], right_ref[0])
        y = both[:total] + (both[total:] + product(x_all[:total], right_ref[1]))
        if len(probes) == 1:
            high, low = split(y)
            r_high[:size], r_high[size : 2 * size], r_high[2 * size :] = high, low, high
            s = product(left_ref[...], r_high[...])
            parts = (s[:size, :size] - s[size:, size:], s[size:, :size] + s[:size, size:])
            for part in range(2):
                leave(0, part, j, parts[part])
            continue
        for n in range(len(probes)):
            rows = slice(n * size, (n + 1) * size)
            r_high[:size, rows], r_low[:size, rows] = split(y[rows, :size])
            r_high[size:, rows], r_low[size:, rows] = split(y[rows, size:])
        both = product(left_ref[...], r_high[...])
        width = 2 * size
        z = both[:width] + (both[width:] + product(left_ref[:width], r_low[...]))
        for n in range(len(probes)):
            rows = slice(n * size, (n + 1) * size)
            for part in range(2):
                leave(n, part, j, z[part * size : (part + 1) * size, rows])


def take(refs, count):
    return [refs.pop(0) for _ in range(count)]


def entry_kernel(layers, groups, base, with_pieces, starts, ends, with_after, *refs):
    refs = list(refs)
    anchors_ref, wave_ref, right_ref, left_ref = take(refs, 4)
    if with_pieces:
        piece_refs = take(refs, 3)
        take(refs, with_after)
        out_refs = take(refs, len(groups))
        ext_refs = take(refs, len(layers))
    else:
        piece_refs = []
        ext_refs = take(refs, len(layers))
        take(refs, with_after)
        out_refs = take(refs, len(groups))
    places = [(g, at) for g, group in enumerate(groups) for at in range(len(group))]

    def put(n, part, wave):
        g, at = places[n]
        out_refs[g][at, part] = wave

    advance(
        0, layers, sum(groups, []), starts, ends, piece_refs, ext_refs, anchors_ref,
        lambda n, part: wave_ref[base + n, part], put, (right_ref, left_ref), refs,
    )


def first_kernel(tick, layers, *refs):
    refs = list(refs)
    anchors_ref, probe_ref, right_ref, left_ref = take(refs, 4)
    ext_refs = take(refs, len(layers))
    _, out_ref = take(refs, 2)
    count = out_ref.shape[0]
    probes = [pl.program_id(0) * count + n for n in range(count)]

    def put(n, part, wave):
        out_ref[n, part] = wave

    @pl.when(lax.axis_index("depth") == 0)
    def _():
        advance(
            tick, layers, probes, True, True, [], ext_refs, anchors_ref,
            lambda n, part: probe_ref[part], put, (right_ref, left_ref), refs,
        )


def tick_kernel(tick, layers, probes, stores, own_store, with_after, *refs):
    refs = list(refs)
    anchors_ref, wave_ref, right_ref, left_ref = take(refs, 4)
    ext_refs = take(refs, len(layers))
    (first_ref,) = take(refs, 1)
    stored_refs = take(refs, len(stores))
    if own_store:
        take(refs, 1 + with_after)
        (final_ref,) = take(refs, 1)
        sem, out_ref = refs.pop(), refs.pop()
    elif stores:
        take(refs, with_after)
        out_ref, final_ref = take(refs, 2)
        sem = refs.pop()
    else:
        take(refs, with_after)
        (out_ref,) = take(refs, 1)

    copies = []
    for n, ((to, at), ref) in enumerate(zip(stores, stored_refs)):
        into = final_ref.at[to, pl.ds(at, ref.shape[0])]
        copies.append(pltpu.make_async_copy(ref, into, sem.at[n]))
        copies[-1].start()

    def put(n, part, wave):
        out_ref[n, part] = wave

    depth = lax.axis_index("depth")

    @pl.when(depth == 0)
    def _():
        out_ref[...] = first_ref[probes[0] : probes[0] + len(probes)]

    @pl.when(depth != 0)
    def _():
        advance(
            tick, layers, probes, True, True, [], ext_refs, anchors_ref,
            lambda n, part: wave_ref[n, part], put, (right_ref, left_ref), refs,
        )

    if own_store:
        into = final_ref.at[tick, pl.ds(probes[0], len(probes))]
        copies.append(pltpu.make_async_copy(out_ref, into, sem.at[len(stores)]))
        copies[-1].start()
    for copy in copies:
        copy.wait()


def vmem():
    return pl.BlockSpec(memory_space=pltpu.VMEM)


def hbm():
    return pl.BlockSpec(memory_space=pltpu.HBM)


def pick(tables, n):
    right, left, single = tables
    return right, single if n == 1 else left


def call(kernel, operands, specs, out_shape, out_specs, n, size, layers, name, **rest):
    grid = rest.pop("grid", (1,))
    flops = WEIGHT * grid[0] * layers * n * 2 * 3 * 2 * size * (2 * size) ** 2
    after = rest.pop("after", None)
    if after is not None:
        operands.append(after)
        specs.append(pl.BlockSpec(memory_space=pl.ANY))
    return pl.pallas_call(
        kernel,
        grid=grid,
        in_specs=specs,
        out_specs=out_specs,
        out_shape=out_shape,
        scratch_shapes=[
            pltpu.VMEM((n, 2, size, size), jnp.float32),
            pltpu.VMEM((2 * n * size, 2 * size), jnp.bfloat16),
            pltpu.VMEM((3 * size, 2 * size) if n == 1 else (2 * size, n * size), jnp.bfloat16),
            pltpu.VMEM((2 * size, n * size), jnp.bfloat16),
            *rest.pop("scratch", []),
        ],
        compiler_params=pltpu.CompilerParams(vmem_limit_bytes=VMEM_LIMIT),
        cost_estimate=pl.CostEstimate(
            flops=flops, bytes_accessed=layers * 2 * 2 * 384 * size * 4, transcendentals=0
        ),
        name=name,
        **rest,
    )(*operands)


def entry(
    layers, groups, anchors, tables, wave, pieces, exts, starts, ends, tile_rows, name, after=None
):
    size = wave.shape[-1]
    count, n = len(layers), sum(map(len, groups))
    base = groups[0][0] if wave.shape[0] != n else 0
    operands = [anchors, wave, *pick(tables, n)]
    specs = [vmem()] * 4
    out_shape = [
        jax.ShapeDtypeStruct((len(group), 2, size, size), jnp.float32) for group in groups
    ]
    if pieces is not None:
        operands += [piece for piece, _ in pieces]
        for _, at in pieces:
            specs.append(
                pl.BlockSpec((count, 2, 2, size, size), lambda i, at=at: (at, 0, 0, 0, 0))
            )
        out_shape += [
            jax.ShapeDtypeStruct((2, 2, tile_rows + size, size), jnp.float32)
        ] * count
    else:
        operands += exts
        specs += [vmem()] * count
    kernel = functools.partial(
        entry_kernel, layers, groups, base, pieces is not None, starts, ends, after is not None
    )
    return call(
        kernel, operands, specs, out_shape, [vmem()] * len(out_shape), n, size, count, name,
        after=after,
    )


def first_section(tick, n, anchors, tables, probe_wave, exts, after, chunks):
    size = probe_wave.shape[-1]
    layers = list(range(len(exts)))
    return call(
        functools.partial(first_kernel, tick, layers),
        [anchors, probe_wave, *pick(tables, n), *exts, after],
        [vmem()] * (4 + len(exts)) + [pl.BlockSpec(memory_space=pl.ANY)],
        jax.ShapeDtypeStruct((chunks * n, 2, size, size), jnp.float32),
        pl.BlockSpec((n, 2, size, size), lambda i: (i, 0, 0, 0)),
        n, size, len(exts), f"first{tick}", grid=(chunks,),
    )


def tick_section(
    tick, probes, anchors, tables, wave, exts, first, after, stored=(), out_shape=None, out=None
):
    size = wave.shape[-1]
    count, n = len(exts), len(probes)
    operands = [anchors, wave, *pick(tables, n), *exts, first, *(part for _, part in stored)]
    specs = [vmem()] * (5 + count + len(stored))
    shape = [jax.ShapeDtypeStruct((n, 2, size, size), jnp.float32)]
    out_specs = [vmem()]
    rest = {"after": after}
    if out is not None:
        rest["input_output_aliases"] = {len(operands): 0}
        operands.append(out)
        specs.append(hbm())
        shape, out_specs = [jax.ShapeDtypeStruct(out.shape, out.dtype)], [hbm()]
        rest["scratch"] = [
            pltpu.VMEM((n, 2, size, size), jnp.float32),
            pltpu.SemaphoreType.DMA((len(stored) + 1,)),
        ]
    elif stored:
        shape.append(out_shape)
        out_specs.append(hbm())
        rest["scratch"] = [pltpu.SemaphoreType.DMA((len(stored),))]
    kernel = functools.partial(
        tick_kernel, tick, list(range(count)), probes, [to for to, _ in stored],
        out is not None, after is not None,
    )
    return call(
        kernel, operands, specs, shape, out_specs, n, size, count, f"tick{tick}_{probes[0]}", **rest
    )


def shards(phase_map, absorb, probe_wave, waves_in, scan_rows, scan_cols):
    size = probe_wave.shape[-1]
    slices, tile_rows = phase_map.shape[:2]
    tiles = lax.axis_size("tile")
    depth_count = lax.axis_size("depth")
    back = [(i, (i - 1) % tiles) for i in range(tiles)]
    onward = [(i, (i + 1) % depth_count) for i in range(depth_count)]

    firsts = edge_rows(phase_map, absorb, size, list(range(slices)))
    rims = [lax.ppermute(first, "tile", back) for first in firsts]
    rest = rest_rows(phase_map, absorb, size)

    tables = [jnp.asarray(table) for table in hop_tables(size)]
    depth, tile = lax.axis_index("depth"), lax.axis_index("tile")
    anchors = jnp.stack([scan_rows - tile * tile_rows, scan_cols], 1)
    anchors = lax.dynamic_slice_in_dim(anchors, depth_count - 1 - depth, TICKS, 0)
    anchors = jnp.broadcast_to(anchors.reshape(-1, 1), (anchors.size, size))
    held = waves_in[0]
    count = held.shape[0]
    exts = []
    done = []
    for r in range(slices):
        layers = [r]
        pieces = [(firsts[r], 0), (rest, r), (rims[r], 0)]
        edges = (r == 0, r == slices - 1, tile_rows)
        if r < slices - 1:
            held, *made = entry(
                layers, [list(range(count))], anchors, tables, held, pieces, None, *edges, f"enter{r}"
            )
            exts += made
            continue
        left, *made = entry(
            layers, GROUPS[:1], anchors, tables, held, pieces, None, *edges, "leave0"
        )
        exts += made
        done = [left]
        done += entry(
            layers, GROUPS[1:], anchors, tables, held, None, exts[-1:], *edges, "leave1", left
        )

    stored = []
    for tick in range(1, TICKS):
        stored += [((tick - 1, group[0]), part) for group, part in zip(GROUPS, done)]
        arrived = [lax.ppermute(left, "depth", onward) for left in done]
        first = first_section(
            tick, 2, anchors, tables, probe_wave, exts, done[-1], count // 2
        )
        done = []
        for c, group in enumerate(GROUPS):
            last = {}
            if tick == TICKS - 1 and c == 0:
                shape = jax.ShapeDtypeStruct((TICKS, count, *held.shape[1:]), held.dtype)
                last = dict(stored=stored, out_shape=shape)
            elif tick == TICKS - 1 and c == len(GROUPS) - 1:
                stored = [((tick, other[0]), part) for other, part in zip(GROUPS, done)]
                last = dict(stored=stored, out=out)
            left, *made = tick_section(
                tick, group, anchors, tables, arrived[c], exts, first,
                done[-1] if done else None, **last
            )
            if made:
                out = made[0]
            done.append(left)
    out = done[-1]
    return out[:, None]


def solution(mesh):
    return jax.shard_map(
        shards,
        mesh=mesh,
        in_specs=(
            P("depth", "tile", None),
            P("depth", "tile", None),
            P(),
            P("depth", "tile", None, None, None),
            P(None, "tile"),
            P(None, "tile"),
        ),
        out_specs=P(None, "depth", "tile", None, None, None),
        check_vma=False,
    )
```

```python
import functools
import math

import jax
import jax.numpy as jnp
import ml_dtypes
import numpy as np
from jax import lax
from jax.experimental import pallas as pl
from jax.experimental.pallas import tpu as pltpu
from jax.sharding import PartitionSpec as P

TICKS = 3
GROUPS = [[0], [1, 2], [3]]

fresnel = 0.1
VMEM_LIMIT = 24 * 1024 * 1024
WEIGHT = 8
EDGE_LIMIT = VMEM_LIMIT

SIN_TERMS = [(-1.0) ** j / math.factorial(2 * j + 1) for j in range(7)]
COS_TERMS = [(-1.0) ** j / math.factorial(2 * j) for j in range(8)]


def hop_tables(size):
    index = np.arange(size)
    frequency = np.where(index < size // 2, index, index - size).astype(np.float64)
    k = np.exp(-1j * fresnel * math.pi * frequency**2 / size)
    lag = np.fft.ifft(k)
    g = lag[(index[:, None] - index[None, :]) % size]
    right = np.block([[g.real, g.imag], [-g.imag, g.real]])
    high = right.astype(ml_dtypes.bfloat16)
    low = (right - high.astype(np.float64)).astype(ml_dtypes.bfloat16)
    right = np.stack([high, low])
    left = right.transpose(0, 2, 1)
    columns = left[:, :, :size]
    single = np.concatenate([columns[0], columns[0], columns[1]], 1)
    return right, left.reshape(4 * size, 2 * size), single


def series(z, terms):
    total = jnp.full_like(z, terms[-1])
    for term in terms[-2::-1]:
        total = total * z + term
    return total


def transmission(phase, absorb):
    t = 0.5 * phase
    z = t * t
    s = t * series(z, SIN_TERMS)
    c = series(z, COS_TERMS)
    damping = jnp.exp(-absorb)
    return damping * (1.0 - 2.0 * (s * s)), damping * (2.0 * (s * c))


def split(x):
    high = x.astype(jnp.bfloat16)
    return high, (x - high.astype(jnp.float32)).astype(jnp.bfloat16)


def product(a, b):
    return jnp.dot(a, b, preferred_element_type=jnp.float32)


def trans_layer(phase_ref, absorb_ref, out_ref):
    rows, columns = phase_ref.shape
    size = out_ref.shape[-1]
    step = 32

    def body(i, carry):
        at = pl.ds(pl.multiple_of(i * step, step), step)
        for half in range(columns // size):
            cols = slice(half * size, (half + 1) * size)
            real, imag = transmission(phase_ref[at, cols], absorb_ref[at, cols])
            out_ref[0, half, at, :] = real
            out_ref[1, half, at, :] = imag
        return carry

    lax.fori_loop(0, rows // step, body, 0)


def edge_kernel(first, phase_ref, absorb_ref, *refs):
    *out_refs, phase_buf, absorb_buf, sem = refs
    count, rows = phase_buf.shape[:2]
    copies = []
    for layer in range(count):
        for n, (ref, buf) in enumerate([(phase_ref, phase_buf), (absorb_ref, absorb_buf)]):
            source = ref.at[first + layer, pl.ds(0, rows)]
            copies.append(pltpu.make_async_copy(source, buf.at[layer], sem.at[2 * layer + n]))
            copies[-1].start()
    for layer in range(count):
        copies[2 * layer].wait()
        copies[2 * layer + 1].wait()
        trans_layer(phase_buf.at[layer], absorb_buf.at[layer], out_refs[layer].at[0])


def rest_kernel(phase_ref, absorb_ref, out_ref):
    for layer in range(phase_ref.shape[0]):
        trans_layer(phase_ref.at[layer], absorb_ref.at[layer], out_ref.at[layer])


def edge_rows(phase_map, absorb, size, layers):
    count, columns = len(layers), phase_map.shape[2]
    shape = jax.ShapeDtypeStruct((1, 2, columns // size, size, size), jnp.float32)
    values = count * size * columns
    return pl.pallas_call(
        functools.partial(edge_kernel, layers[0]),
        out_shape=[shape] * count,
        in_specs=[hbm()] * 2,
        out_specs=[vmem()] * count,
        scratch_shapes=[
            pltpu.VMEM((count, size, columns), jnp.float32),
            pltpu.VMEM((count, size, columns), jnp.float32),
            pltpu.SemaphoreType.DMA((2 * count,)),
        ],
        compiler_params=pltpu.CompilerParams(vmem_limit_bytes=EDGE_LIMIT),
        cost_estimate=pl.CostEstimate(
            flops=values * 40, bytes_accessed=values * 16, transcendentals=values
        ),
        name=f"edge{layers[0]}",
    )(*(pltpu.with_memory_space_constraint(x, pltpu.HBM) for x in (phase_map, absorb)))


def rest_rows(phase_map, absorb, size):
    count, rows, columns = phase_map.shape
    spec = pl.BlockSpec((count, rows - size, columns), lambda i: (0, 1, 0))
    values = count * (rows - size) * columns
    return pl.pallas_call(
        rest_kernel,
        grid=(1,),
        out_shape=jax.ShapeDtypeStruct((count, 2, columns // size, rows - size, size), jnp.float32),
        in_specs=[spec] * 2,
        out_specs=vmem(),
        compiler_params=pltpu.CompilerParams(vmem_limit_bytes=VMEM_LIMIT),
        cost_estimate=pl.CostEstimate(
            flops=values * 40, bytes_accessed=values * 16, transcendentals=values
        ),
        name="rest",
    )(phase_map, absorb)


def advance(
    tick, layers, probes, starts, ends, piece_refs, ext_refs, anchors_ref, waves, put, tables, scratch
):
    right_ref, left_ref = tables
    state, x_all, r_high, r_low = scratch
    size = state.shape[-1]
    each = anchors_ref.shape[0] // (2 * TICKS)
    row_at, col_at = [
        [anchors_ref[pl.ds((2 * tick + axis) * each + p, 1), :][0, 0] for p in probes]
        for axis in range(2)
    ]
    lane = lax.broadcasted_iota(jnp.int32, (size, size), 1)
    count, total = len(layers), len(probes) * size

    for n in range(len(probes)):
        for part in range(2):
            wave = waves(n, part)
            if starts:
                wave = pltpu.roll(wave, col_at[n] & (size - 1), 1)
            state[n, part] = wave

    def leave(n, part, j, wave):
        if j < count - 1:
            state[n, part] = wave
            return
        if ends:
            wave = pltpu.roll(wave, (size - col_at[n]) & (size - 1), 1)
        put(n, part, wave)

    for j in range(count):
        ext = ext_refs[j]
        for piece, piece_ref in enumerate(piece_refs):
            rows = slice(piece * size, (piece + 1) * size)
            for part in range(2):
                for half in range(2):
                    ext[part, half, rows, :] = piece_ref[j, part, half]
        for n in range(len(probes)):
            at = pl.ds(row_at[n], size)
            inside = lane >= col_at[n]
            t_real = jnp.where(inside, ext[0, 0, at, :], ext[0, 1, at, :])
            t_imag = jnp.where(inside, ext[1, 0, at, :], ext[1, 1, at, :])
            real, imag = state[n, 0], state[n, 1]
            rows = slice(n * size, (n + 1) * size)
            lows = slice(total + n * size, total + (n + 1) * size)
            x_all[rows, :size], x_all[lows, :size] = split(real * t_real - imag * t_imag)
            x_all[rows, size:], x_all[lows, size:] = split(real * t_imag + imag * t_real)
        both = product(x_all[...], right_ref[0])
        y = both[:total] + (both[total:] + product(x_all[:total], right_ref[1]))
        if len(probes) == 1:
            high, low = split(y)
            r_high[:size], r_high[size : 2 * size], r_high[2 * size :] = high, low, high
            s = product(left_ref[...], r_high[...])
            parts = (s[:size, :size] - s[size:, size:], s[size:, :size] + s[:size, size:])
            for part in range(2):
                leave(0, part, j, parts[part])
            continue
        for n in range(len(probes)):
            rows = slice(n * size, (n + 1) * size)
            r_high[:size, rows], r_low[:size, rows] = split(y[rows, :size])
            r_high[size:, rows], r_low[size:, rows] = split(y[rows, size:])
        both = product(left_ref[...], r_high[...])
        width = 2 * size
        z = both[:width] + (both[width:] + product(left_ref[:width], r_low[...]))
        for n in range(len(probes)):
            rows = slice(n * size, (n + 1) * size)
            for part in range(2):
                leave(n, part, j, z[part * size : (part + 1) * size, rows])


def take(refs, count):
    return [refs.pop(0) for _ in range(count)]


def entry_kernel(layers, groups, base, with_pieces, starts, ends, with_after, *refs):
    refs = list(refs)
    anchors_ref, wave_ref, right_ref, left_ref = take(refs, 4)
    if with_pieces:
        piece_refs = take(refs, 3)
        take(refs, with_after)
        out_refs = take(refs, len(groups))
        ext_refs = take(refs, len(layers))
    else:
        piece_refs = []
        ext_refs = take(refs, len(layers))
        take(refs, with_after)
        out_refs = take(refs, len(groups))
    places = [(g, at) for g, group in enumerate(groups) for at in range(len(group))]

    def put(n, part, wave):
        g, at = places[n]
        out_refs[g][at, part] = wave

    advance(
        0, layers, sum(groups, []), starts, ends, piece_refs, ext_refs, anchors_ref,
        lambda n, part: wave_ref[base + n, part], put, (right_ref, left_ref), refs,
    )


def first_kernel(tick, layers, *refs):
    refs = list(refs)
    anchors_ref, probe_ref, right_ref, left_ref = take(refs, 4)
    ext_refs = take(refs, len(layers))
    _, out_ref = take(refs, 2)
    count = out_ref.shape[0]
    probes = [pl.program_id(0) * count + n for n in range(count)]

    def put(n, part, wave):
        out_ref[n, part] = wave

    @pl.when(lax.axis_index("depth") == 0)
    def _():
        advance(
            tick, layers, probes, True, True, [], ext_refs, anchors_ref,
            lambda n, part: probe_ref[part], put, (right_ref, left_ref), refs,
        )


def tick_kernel(tick, layers, probes, stores, own_store, with_after, *refs):
    refs = list(refs)
    anchors_ref, wave_ref, right_ref, left_ref = take(refs, 4)
    ext_refs = take(refs, len(layers))
    (first_ref,) = take(refs, 1)
    stored_refs = take(refs, len(stores))
    if own_store:
        take(refs, 1 + with_after)
        (final_ref,) = take(refs, 1)
        sem, out_ref = refs.pop(), refs.pop()
    elif stores:
        take(refs, with_after)
        out_ref, final_ref = take(refs, 2)
        sem = refs.pop()
    else:
        take(refs, with_after)
        (out_ref,) = take(refs, 1)

    copies = []
    for n, ((to, at), ref) in enumerate(zip(stores, stored_refs)):
        into = final_ref.at[to, pl.ds(at, ref.shape[0])]
        copies.append(pltpu.make_async_copy(ref, into, sem.at[n]))
        copies[-1].start()

    def put(n, part, wave):
        out_ref[n, part] = wave

    depth = lax.axis_index("depth")

    @pl.when(depth == 0)
    def _():
        out_ref[...] = first_ref[probes[0] : probes[0] + len(probes)]

    @pl.when(depth != 0)
    def _():
        advance(
            tick, layers, probes, True, True, [], ext_refs, anchors_ref,
            lambda n, part: wave_ref[n, part], put, (right_ref, left_ref), refs,
        )

    if own_store:
        into = final_ref.at[tick, pl.ds(probes[0], len(probes))]
        copies.append(pltpu.make_async_copy(out_ref, into, sem.at[len(stores)]))
        copies[-1].start()
    for copy in copies:
        copy.wait()


def vmem():
    return pl.BlockSpec(memory_space=pltpu.VMEM)


def hbm():
    return pl.BlockSpec(memory_space=pltpu.HBM)


def pick(tables, n):
    right, left, single = tables
    return right, single if n == 1 else left


def call(kernel, operands, specs, out_shape, out_specs, n, size, layers, name, **rest):
    grid = rest.pop("grid", (1,))
    flops = WEIGHT * grid[0] * layers * n * 2 * 3 * 2 * size * (2 * size) ** 2
    after = rest.pop("after", None)
    if after is not None:
        operands.append(after)
        specs.append(pl.BlockSpec(memory_space=pl.ANY))
    return pl.pallas_call(
        kernel,
        grid=grid,
        in_specs=specs,
        out_specs=out_specs,
        out_shape=out_shape,
        scratch_shapes=[
            pltpu.VMEM((n, 2, size, size), jnp.float32),
            pltpu.VMEM((2 * n * size, 2 * size), jnp.bfloat16),
            pltpu.VMEM((3 * size, 2 * size) if n == 1 else (2 * size, n * size), jnp.bfloat16),
            pltpu.VMEM((2 * size, n * size), jnp.bfloat16),
            *rest.pop("scratch", []),
        ],
        compiler_params=pltpu.CompilerParams(vmem_limit_bytes=VMEM_LIMIT),
        cost_estimate=pl.CostEstimate(
            flops=flops, bytes_accessed=layers * 2 * 2 * 384 * size * 4, transcendentals=0
        ),
        name=name,
        **rest,
    )(*operands)


def entry(
    layers, groups, anchors, tables, wave, pieces, exts, starts, ends, tile_rows, name, after=None
):
    size = wave.shape[-1]
    count, n = len(layers), sum(map(len, groups))
    base = groups[0][0] if wave.shape[0] != n else 0
    operands = [anchors, wave, *pick(tables, n)]
    specs = [vmem()] * 4
    out_shape = [
        jax.ShapeDtypeStruct((len(group), 2, size, size), jnp.float32) for group in groups
    ]
    if pieces is not None:
        operands += [piece for piece, _ in pieces]
        for _, at in pieces:
            specs.append(
                pl.BlockSpec((count, 2, 2, size, size), lambda i, at=at: (at, 0, 0, 0, 0))
            )
        out_shape += [
            jax.ShapeDtypeStruct((2, 2, tile_rows + size, size), jnp.float32)
        ] * count
    else:
        operands += exts
        specs += [vmem()] * count
    kernel = functools.partial(
        entry_kernel, layers, groups, base, pieces is not None, starts, ends, after is not None
    )
    return call(
        kernel, operands, specs, out_shape, [vmem()] * len(out_shape), n, size, count, name,
        after=after,
    )


def first_section(tick, n, anchors, tables, probe_wave, exts, after, chunks):
    size = probe_wave.shape[-1]
    layers = list(range(len(exts)))
    return call(
        functools.partial(first_kernel, tick, layers),
        [anchors, probe_wave, *pick(tables, n), *exts, after],
        [vmem()] * (4 + len(exts)) + [pl.BlockSpec(memory_space=pl.ANY)],
        jax.ShapeDtypeStruct((chunks * n, 2, size, size), jnp.float32),
        pl.BlockSpec((n, 2, size, size), lambda i: (i, 0, 0, 0)),
        n, size, len(exts), f"first{tick}", grid=(chunks,),
    )


def tick_section(
    tick, probes, anchors, tables, wave, exts, first, after, stored=(), out_shape=None, out=None
):
    size = wave.shape[-1]
    count, n = len(exts), len(probes)
    operands = [anchors, wave, *pick(tables, n), *exts, first, *(part for _, part in stored)]
    specs = [vmem()] * (5 + count + len(stored))
    shape = [jax.ShapeDtypeStruct((n, 2, size, size), jnp.float32)]
    out_specs = [vmem()]
    rest = {"after": after}
    if out is not None:
        rest["input_output_aliases"] = {len(operands): 0}
        operands.append(out)
        specs.append(hbm())
        shape, out_specs = [jax.ShapeDtypeStruct(out.shape, out.dtype)], [hbm()]
        rest["scratch"] = [
            pltpu.VMEM((n, 2, size, size), jnp.float32),
            pltpu.SemaphoreType.DMA((len(stored) + 1,)),
        ]
    elif stored:
        shape.append(out_shape)
        out_specs.append(hbm())
        rest["scratch"] = [pltpu.SemaphoreType.DMA((len(stored),))]
    kernel = functools.partial(
        tick_kernel, tick, list(range(count)), probes, [to for to, _ in stored],
        out is not None, after is not None,
    )
    return call(
        kernel, operands, specs, shape, out_specs, n, size, count, f"tick{tick}_{probes[0]}", **rest
    )


def shards(phase_map, absorb, probe_wave, waves_in, scan_rows, scan_cols):
    size = probe_wave.shape[-1]
    slices, tile_rows = phase_map.shape[:2]
    tiles = lax.axis_size("tile")
    depth_count = lax.axis_size("depth")
    back = [(i, (i - 1) % tiles) for i in range(tiles)]
    onward = [(i, (i + 1) % depth_count) for i in range(depth_count)]

    firsts = edge_rows(phase_map, absorb, size, [0])
    firsts += edge_rows(phase_map, absorb, size, list(range(1, slices)))
    rims = [lax.ppermute(first, "tile", back) for first in firsts]
    rest = rest_rows(phase_map, absorb, size)

    tables = [jnp.asarray(table) for table in hop_tables(size)]
    depth, tile = lax.axis_index("depth"), lax.axis_index("tile")
    anchors = jnp.stack([scan_rows - tile * tile_rows, scan_cols], 1)
    anchors = lax.dynamic_slice_in_dim(anchors, depth_count - 1 - depth, TICKS, 0)
    anchors = jnp.broadcast_to(anchors.reshape(-1, 1), (anchors.size, size))
    held = waves_in[0]
    count = held.shape[0]
    exts = []
    done = []
    for r in range(slices):
        layers = [r]
        pieces = [(firsts[r], 0), (rest, r), (rims[r], 0)]
        edges = (r == 0, r == slices - 1, tile_rows)
        if r < slices - 1:
            held, *made = entry(
                layers, [list(range(count))], anchors, tables, held, pieces, None, *edges, f"enter{r}"
            )
            exts += made
            continue
        left, *made = entry(
            layers, GROUPS[:1], anchors, tables, held, pieces, None, *edges, "leave0"
        )
        exts += made
        done = [left]
        done += entry(
            layers, GROUPS[1:], anchors, tables, held, None, exts[-1:], *edges, "leave1", left
        )

    stored = []
    for tick in range(1, TICKS):
        stored += [((tick - 1, group[0]), part) for group, part in zip(GROUPS, done)]
        arrived = [lax.ppermute(left, "depth", onward) for left in done]
        first = first_section(
            tick, 2, anchors, tables, probe_wave, exts, done[-1], count // 2
        )
        done = []
        for c, group in enumerate(GROUPS):
            last = {}
            if tick == TICKS - 1 and c == 0:
                shape = jax.ShapeDtypeStruct((TICKS, count, *held.shape[1:]), held.dtype)
                last = dict(stored=stored, out_shape=shape)
            elif tick == TICKS - 1 and c == len(GROUPS) - 1:
                stored = [((tick, other[0]), part) for other, part in zip(GROUPS, done)]
                last = dict(stored=stored, out=out)
            left, *made = tick_section(
                tick, group, anchors, tables, arrived[c], exts, first,
                done[-1] if done else None, **last
            )
            if made:
                out = made[0]
            done.append(left)
    out = done[-1]
    return out[:, None]


def solution(mesh):
    return jax.shard_map(
        shards,
        mesh=mesh,
        in_specs=(
            P("depth", "tile", None),
            P("depth", "tile", None),
            P(),
            P("depth", "tile", None, None, None),
            P(None, "tile"),
            P(None, "tile"),
        ),
        out_specs=P(None, "depth", "tile", None, None, None),
        check_vma=False,
    )
```
